256 devices in a mesh: rows: 32 (over x_lo, z, core), cols: 8 (over y, x_hi).
Axes of the slice: x: 4 (x_hi: 2, x_lo: 2; x = x_hi * 2 + x_lo), y: 4, z: 8, core: 2. Of those that a mesh axis runs over, the one named last changes fastest.
Arguments:
- current_frame: bfloat16 [128, 512, 1024], P(None, 'rows', 'cols'), may hold values from -6 to 6
- history_frames: bfloat16 [3, 128, 512, 1024], P(None, None, 'rows', 'cols'), may hold values from -6 to 6
- offsets: int32 [3, 2], replicated, may hold values from -16 to 16, as said below
- compress_weight: bfloat16 [32, 128], replicated, may hold values from -0.5 to 0.5
- mixer_weight: bfloat16 [3, 3, 128, 224], replicated, may hold values from -0.125 to 0.125
- mixer_bias: float32 [128], replicated, may hold values from -3 to 3
Outputs:
- joined_grid: bfloat16 [128, 512, 1024], P(None, 'rows', 'cols')
The draws below stay inside these ranges and needn't reach their ends.
Inputs may be any that keep to these rules, and one draw needn't show every extreme that they name: offsets[k, 0] lies in -8..8 and offsets[k, 1] in -16..16; no offset is 0; in each of the two columns one frame's offset equals the bound and another equals its negative.
All inputs are finite; a program needn't handle non-finite values.
Results may differ from the reference program's by a relative error of at most 0.0034.
Values may be sent and summed in bfloat16 or wider, within the bound.
No kernel may reach another device: no remote copies, remote signals or barrier semaphores. Data moves between devices by JAX's collectives and lax.ppermute only.
A program may use at most 64 MiB of HBM per device.

```python
import jax
import jax.numpy as jnp
from jax import lax

C = 128
CP = 32
FRAMES = 3
CR = 16
SHIFT_X = 16
SHIFT_Y = 8
GRID_ROWS = 512
GRID_COLS = 1024


def offset_column(key, bound):
    key_mags, key_sign, key_perm = jax.random.split(key, 3)
    spare_mag = jax.random.randint(key_mags, (), 1, bound + 1)
    mags = jnp.stack([jnp.int32(bound), jnp.int32(bound), spare_mag.astype(jnp.int32)])
    spare = 2 * jax.random.randint(key_sign, (), 0, 2) - 1
    signs = jnp.stack([jnp.int32(1), jnp.int32(-1), spare.astype(jnp.int32)])
    order = jax.random.permutation(key_perm, jnp.arange(3, dtype=jnp.int32))
    return (mags * signs)[order]


def draw_offsets(key, part):
    key_rows = jax.random.fold_in(key, 11)
    key_cols = jax.random.fold_in(key, 23)
    return jnp.stack([offset_column(key_rows, SHIFT_Y), offset_column(key_cols, SHIFT_X)], axis=1).astype(jnp.int32)


def block_scale(stream_key, extent, shards, low, largest):
    gain = 1.0
    for axis_at, parts in shards:
        draws = jax.random.uniform(jax.random.fold_in(jax.random.fold_in(stream_key, 6), axis_at), (parts,), jnp.float32, low / len(shards), largest / len(shards))
        gain = gain * jnp.repeat(jnp.exp(draws), extent[axis_at] // parts).reshape((-1,) + (1,) * (len(extent) - 1 - axis_at))
    return gain


def noise(key, dims, scale, reach, cuts=(), kind=jnp.bfloat16):
    drawn = scale * jax.random.normal(key, dims, jnp.float32)
    if cuts:
        drawn = drawn * block_scale(key, dims, cuts, -0.22, 0.18)
    return jnp.clip(drawn, -reach, reach).astype(kind)


def setup_inputs(seed: int = 0) -> dict:
    key_list = jax.random.split(jax.random.key(seed), 7)
    return {
        "current_frame": noise(key_list[0], (C, GRID_ROWS, GRID_COLS), 1.0, 6.0, ((1, 32), (2, 8))),
        "history_frames": noise(key_list[1], (FRAMES, C, GRID_ROWS, GRID_COLS), 1.0, 6.0, ((2, 32), (3, 8))),
        "offsets": draw_offsets(jax.random.fold_in(key_list[6], 71), 0),
        "compress_weight": noise(key_list[3], (CP, C), C ** -0.5, 0.5),
        "mixer_weight": noise(key_list[4], (3, 3, C, C + FRAMES * CP), (9 * (C + FRAMES * CP)) ** -0.5, 0.125),
        "mixer_bias": noise(key_list[5], (C,), 0.5, 3.0, (), jnp.float32),
    }


def shift_frame(frame, row_offset, col_offset):
    padded = jnp.pad(frame, ((0, 0), (SHIFT_Y, SHIFT_Y), (SHIFT_X, SHIFT_X)))
    starts = (jnp.int32(0), (SHIFT_Y - row_offset).astype(jnp.int32), (SHIFT_X - col_offset).astype(jnp.int32))
    return lax.dynamic_slice(padded, starts, (CP, GRID_ROWS, GRID_COLS))


def conv_taps(present_rows, older_rows, mixer_weight, mixer_bias):
    height = present_rows.shape[1] - 2
    width = present_rows.shape[2] - 2
    channels = present_rows.shape[0]
    total = jnp.zeros((mixer_weight.shape[2], height * width), jnp.float32)
    for tap_row in range(3):
        for tap_col in range(3):
            present = present_rows[:, tap_row:tap_row + height, tap_col:tap_col + width].reshape(channels, -1)
            older = older_rows[:, tap_row:tap_row + height, tap_col:tap_col + width].reshape(older_rows.shape[0], -1)
            total = total + jnp.dot(mixer_weight[tap_row, tap_col, :, :channels], present, preferred_element_type=jnp.float32)
            total = total + jnp.dot(mixer_weight[tap_row, tap_col, :, channels:], older, preferred_element_type=jnp.float32)
    result = jnp.maximum(total + mixer_bias[:, None], 0.0)
    return result.astype(jnp.bfloat16).reshape(-1, height, width)


def reference(current_frame, history_frames, offsets, compress_weight, mixer_weight, mixer_bias):
    pieces = []
    for frame_index in range(FRAMES):
        flattened = history_frames[frame_index].reshape(C, -1)
        reduced = jnp.dot(compress_weight, flattened, preferred_element_type=jnp.float32).astype(jnp.bfloat16)
        reduced = reduced.reshape(CP, GRID_ROWS, GRID_COLS)
        pieces.append(shift_frame(reduced, offsets[frame_index, 0], offsets[frame_index, 1]))
    shifted = jnp.concatenate(pieces, axis=0)
    present_pad = jnp.pad(current_frame, ((0, 0), (1, 1), (1, 1)))
    older_pad = jnp.pad(shifted, ((0, 0), (1, 1), (1, 1)))

    def row_block(block_index):
        row_start = (block_index * CR).astype(jnp.int32)
        present_rows = lax.dynamic_slice_in_dim(present_pad, row_start, CR + 2, 1)
        older_rows = lax.dynamic_slice_in_dim(older_pad, row_start, CR + 2, 1)
        return conv_taps(present_rows, older_rows, mixer_weight, mixer_bias)

    blocks = lax.map(row_block, jnp.arange(GRID_ROWS // CR, dtype=jnp.int32))
    return blocks.transpose(1, 0, 2, 3).reshape(C, GRID_ROWS, GRID_COLS)
```

```python
import jax
import jax.numpy as jnp
from jax import lax
from jax.experimental import pallas as pl
from jax.experimental.pallas import tpu as pltpu
from jax.sharding import PartitionSpec as P

C = 128
CP = 32
FRAMES = 3
CR = 16
CC = 128
SHIFT_X = 16
SHIFT_Y = 8
REACH = SHIFT_Y + 1
WIN = CR + 2
KROW = 3 * C + 3 * FRAMES * CP
KALL = 2048
TILES = 3
SEG = 21
SEG0 = CC - SEG
VMEM_LIMIT = 48 * 1024 * 1024
f32 = jnp.float32
bf16 = jnp.bfloat16


def slots(off, axis):
    pos = [off[axis, k] > 0 for k in range(FRAMES)]
    first_pos = jnp.where(pos[0], 0, jnp.where(pos[1], 1, 2))
    last_pos = jnp.where(pos[2], 2, jnp.where(pos[1], 1, 0))
    first_neg = jnp.where(pos[0], jnp.where(pos[1], 2, 1), 0)
    last_neg = jnp.where(pos[2], jnp.where(pos[1], 0, 1), 2)
    place = [
        jnp.where(pos[k], jnp.where(first_pos == k, 0, 1), jnp.where(first_neg == k, 0, 1))
        for k in range(FRAMES)
    ]
    return pos, (first_pos, last_pos), (first_neg, last_neg), place


def lanes(shape):
    return lax.broadcasted_iota(jnp.int32, shape, len(shape) - 1)


def compress_kernel(off, hist, cur, w, red, send_a, send_b, hbuf, cbuf, fbuf, sems):
    copies = [pltpu.make_async_copy(hist.at[k], hbuf.at[k], sems.at[k]) for k in range(FRAMES)]
    copies.append(pltpu.make_async_copy(cur, cbuf, sems.at[FRAMES]))
    for copy in copies:
        copy.start()
    row = lax.axis_index("rows")
    even = row % 2 == 0
    for k in range(FRAMES):
        copies[k].wait()
        fbuf[k] = hbuf[k].astype(f32)
        x = jnp.concatenate(
            [fbuf[k, pl.ds(y, C, stride=CR), :].astype(bf16) for y in range(CR)], axis=1
        )
        r = jnp.dot(w[...], x, preferred_element_type=f32).astype(bf16)
        for y in range(CR):
            red[k, y] = r[:, y * CC : (y + 1) * CC]
    copies[FRAMES].wait()
    fbuf[0] = cbuf[...].astype(f32)
    top = fbuf[0, pl.ds(0, C, stride=CR), :].astype(bf16).reshape(C // CP, CP, CC)
    bottom = fbuf[0, pl.ds(CR - 1, C, stride=CR), :].astype(bf16).reshape(C // CP, CP, CC)
    _, posf, negf, _ = slots(off, 0)
    for send, down in ((send_a, even), (send_b, jnp.logical_not(even))):
        start = jnp.where(down, CR - REACH, 0)
        for s in range(2):
            k = jnp.where(down, posf[s], negf[s])
            for i in range(REACH):
                send[s * REACH + i] = red[k, start + i]
        send[2 * REACH : 2 * REACH + C // CP] = jnp.where(down, bottom, top)


def prepare_kernel(cur, wt, cur_t, cols, wall, fbuf):
    fbuf[...] = cur[...].astype(f32)
    lane = lanes((C, CC))
    first = jnp.zeros((C, CC), f32)
    last = jnp.zeros((C, CC), f32)
    for y in range(CR):
        t = fbuf[pl.ds(y, C, stride=CR), :]
        cur_t[y] = t.astype(bf16)
        first = jnp.where(lane == y + 1, pltpu.roll(t, y + 1, 1), first)
        last = jnp.where(lane == y + 1, pltpu.roll(t, y + 2, 1), last)
    cols[0] = first.astype(bf16)
    cols[1] = last.astype(bf16)
    parts = []
    for i in range(3):
        parts += [wt[i, j, :C, :] for j in range(3)]
        parts += [wt[i, j, C:, :] for j in range(3)]
    parts.append(jnp.zeros((KALL - 3 * KROW, C), bf16))
    tall = jnp.concatenate(parts, axis=0).astype(f32)
    for b in range(KALL // C):
        wall[:, b * C : (b + 1) * C] = tall[b * C : (b + 1) * C].T.astype(bf16)


def window_kernel(nrows, off, red, recv_a, recv_b, cols, win, edge, send_a, send_b, cb):
    row = lax.axis_index("rows")
    col = lax.axis_index("cols")
    even = row % 2 == 0
    has_above = row > 0
    has_below = row < nrows - 1
    pos, _, _, place = slots(off, 0)
    zero = jnp.zeros((REACH, CP, CC), bf16)
    for k in range(FRAMES):
        cb[k, REACH : REACH + CR] = red[k]
        at = pl.ds(place[k] * REACH, REACH)
        from_a = recv_a[at]
        from_b = recv_b[at]
        use_a = jnp.logical_xor(pos[k], even)
        ok = jnp.where(pos[k], has_above, has_below)
        halo = jnp.where(ok, jnp.where(use_a, from_a, from_b), zero)
        cb[k, pl.ds(jnp.where(pos[k], 0, REACH + CR), REACH)] = halo
    for k in range(FRAMES):
        start = SHIFT_Y - off[0, k]
        for r in range(WIN):
            v = cb[k, start + r]
            if r == 0:
                v = jnp.where(has_above, v, jnp.zeros_like(v))
            if r == WIN - 1:
                v = jnp.where(has_below, v, jnp.zeros_like(v))
            win[k, r] = v
    tail_a = recv_a[2 * REACH : 2 * REACH + C // CP].reshape(C, CC)
    tail_b = recv_b[2 * REACH : 2 * REACH + C // CP].reshape(C, CC)
    blank = jnp.zeros((C, CC), bf16)
    above = jnp.where(has_above, jnp.where(even, tail_b, tail_a), blank)
    below = jnp.where(has_below, jnp.where(even, tail_a, tail_b), blank)
    edge[0] = above
    edge[1] = below
    above = above.astype(f32)
    below = below.astype(f32)
    ceven = col % 2 == 0
    _, posf, negf, _ = slots(off, 1)
    lane = lanes((CP, CC))
    wide = lanes((C, CC))
    first = jnp.where(wide == 0, above, cols[0].astype(f32))
    first = jnp.where(wide == WIN - 1, pltpu.roll(below, WIN - 1, 1), first)
    last = jnp.where(wide == 0, pltpu.roll(above, 1, 1), cols[1].astype(f32))
    last = jnp.where(wide == WIN - 1, pltpu.roll(below, WIN, 1), last)
    for send, right in ((send_a, ceven), (send_b, jnp.logical_not(ceven))):
        back = jnp.where(right, SEG0, 0)
        for s in range(2):
            k = jnp.where(right, posf[s], negf[s])
            for t in range(TILES):
                total = jnp.zeros((CP, CC), f32)
                for q in range(WIN // TILES):
                    piece = win[k, t + TILES * q].astype(f32)
                    piece = pltpu.roll(piece, (SEG * q - back + CC) % CC, 1)
                    total = jnp.where((lane >= SEG * q) & (lane < SEG * (q + 1)), piece, total)
                send[s * TILES + t] = total.astype(bf16)
        pack = jnp.where(right, last, first)
        total = pack[:CP]
        for g in range(1, C // CP):
            total = jnp.where(lane >= CP * g, pltpu.roll(pack[CP * g : CP * (g + 1)], CP * g, 1), total)
        send[2 * TILES] = total.astype(bf16)


def join_kernel(ncols, off, win, edge, cur_t, recv_a, recv_b, wall, bias, out, x2, acc):
    col = lax.axis_index("cols")
    ceven = col % 2 == 0
    has_left = col > 0
    has_right = col < ncols - 1
    pos, _, _, place = slots(off, 1)
    lane = lanes((CP, CC))
    wide = lanes((C, CC))

    def unpack(ref):
        t = ref[2 * TILES].astype(f32)
        return jnp.concatenate(
            [t] + [pltpu.roll(t, CC - CP * g, 1) for g in range(1, C // CP)], axis=0
        )

    pack_a = unpack(recv_a)
    pack_b = unpack(recv_b)
    left = jnp.where(ceven, pack_b, pack_a)
    right = jnp.where(ceven, pack_a, pack_b)
    left = jnp.where(has_left, left, jnp.zeros_like(left))
    right = jnp.where(has_right, right, jnp.zeros_like(right))

    def put(r, at, size, value):
        if r <= WIN - CR // 2 - 1:
            x2[r * KROW + at : r * KROW + at + size, :CC] = value
        if r >= CR // 2:
            q = r - CR // 2
            x2[q * KROW + at : q * KROW + at + size, CC:] = value

    for r in range(WIN):
        if r == 0:
            here = edge[0]
        elif r == WIN - 1:
            here = edge[1]
        else:
            here = cur_t[r - 1]
        put(r, C, C, here)
        here = here.astype(f32)
        before = jnp.where(wide == 0, pltpu.roll(left, (CC - r) % CC, 1), pltpu.roll(here, 1, 1))
        after = jnp.where(
            wide == CC - 1, pltpu.roll(right, CC - 1 - r, 1), pltpu.roll(here, CC - 1, 1)
        )
        put(r, 0, C, before.astype(bf16))
        put(r, 2 * C, C, after.astype(bf16))
    for k in range(FRAMES):
        use_a = jnp.logical_xor(pos[k], ceven)
        ok = jnp.where(pos[k], has_left, has_right)
        back = jnp.where(pos[k], SEG0, 0)
        tiles = []
        for t in range(TILES):
            a = recv_a[place[k] * TILES + t].astype(f32)
            b = recv_b[place[k] * TILES + t].astype(f32)
            v = jnp.where(use_a, a, b)
            tiles.append(jnp.where(ok, v, jnp.zeros_like(v)))
        taps = []
        for j in range(3):
            s = off[1, k] + 1 - j
            lo = jnp.where(pos[k], CC - s, 0)
            hi = jnp.where(pos[k], CC, -s)
            mask = (lane >= lo) & (lane < hi)
            outside = None
            if j == 0:
                outside = jnp.logical_and(lane == 0, jnp.logical_not(has_left))
            if j == 2:
                outside = jnp.logical_and(lane == CC - 1, jnp.logical_not(has_right))
            taps.append(((s + CC) % CC, mask, outside))
        for r in range(WIN):
            t, q = r % TILES, r // TILES
            local = win[k, r].astype(f32)
            halo = pltpu.roll(tiles[t], (back - SEG * q + CC) % CC, 1)
            for j in range(3):
                s, mask, outside = taps[j]
                v = pltpu.roll(jnp.where(mask, halo, local), s, 1)
                if outside is not None:
                    v = jnp.where(outside, jnp.zeros_like(v), v)
                put(r, 3 * C + j * FRAMES * CP + k * CP, CP, v.astype(bf16))
    x2[(WIN - CR // 2) * KROW :, :] = jnp.zeros((KALL - 3 * KROW, 2 * CC), bf16)
    bias_col = jnp.broadcast_to(bias[...], (C, 2 * CC))
    for y in range(CR // 2):
        p = jnp.dot(
            wall[...], x2[y * KROW : y * KROW + KALL, :], preferred_element_type=f32
        )
        p = jnp.maximum(p + bias_col, 0.0)
        acc[pl.ds(y, C, stride=CR), :] = p[:, :CC]
        acc[pl.ds(y + CR // 2, C, stride=CR), :] = p[:, CC:]
    out[...] = acc[...].astype(bf16)


def swap(x, axis, shifted):
    size = lax.axis_size(axis)
    if shifted:
        pairs = [(i, (i - 1 if i % 2 == 0 else i + 1) % size) for i in range(size)]
    else:
        pairs = [(i, i ^ 1) for i in range(size)]
    return lax.ppermute(x, axis, pairs)


def cost(flops, bytes_accessed):
    return pl.CostEstimate(flops=flops, bytes_accessed=bytes_accessed, transcendentals=0)


def call(kernel, outs, specs, scratch, estimate):
    vmem = pl.BlockSpec(memory_space=pltpu.VMEM)
    return pl.pallas_call(
        kernel,
        out_shape=[jax.ShapeDtypeStruct(shape, bf16) for shape in outs],
        in_specs=specs,
        out_specs=[vmem] * len(outs),
        scratch_shapes=scratch,
        cost_estimate=estimate,
        compiler_params=pltpu.CompilerParams(vmem_limit_bytes=VMEM_LIMIT),
    )


def body(current_frame, history_frames, offsets, compress_weight, mixer_weight, mixer_bias):
    smem = pl.BlockSpec(memory_space=pltpu.SMEM)
    vmem = pl.BlockSpec(memory_space=pltpu.VMEM)
    hbm = pl.BlockSpec(memory_space=pl.ANY)
    off = offsets.T
    hist = history_frames.reshape(FRAMES, C * CR, CC)
    cur = current_frame.reshape(C * CR, CC)
    wt = mixer_weight.transpose(0, 1, 3, 2)
    nrows, ncols = lax.axis_size("rows"), lax.axis_size("cols")
    row_send = (2 * REACH + C // CP, CP, CC)
    col_send = (2 * TILES + 1, CP, CC)
    red, send_a, send_b = call(
        compress_kernel,
        [(FRAMES, CR, CP, CC), row_send, row_send],
        [smem, hbm, hbm, vmem],
        [
            pltpu.VMEM((FRAMES, C * CR, CC), bf16),
            pltpu.VMEM((C * CR, CC), bf16),
            pltpu.VMEM((FRAMES, C * CR, CC), f32),
            pltpu.SemaphoreType.DMA((FRAMES + 1,)),
        ],
        cost(2 * FRAMES * CP * C * CR * CC, 3 << 20),
    )(off, hist, cur, compress_weight)
    recv_a = swap(send_a, "rows", False)
    recv_b = swap(send_b, "rows", True)
    cur_t, cols, wall = call(
        prepare_kernel,
        [(CR, C, CC), (2, C, CC), (C, KALL)],
        [vmem, vmem],
        [pltpu.VMEM((C * CR, CC), f32)],
        cost(1 << 20, 3 << 20),
    )(cur, wt)
    win, edge, send_a, send_b = call(
        lambda *refs: window_kernel(nrows, *refs),
        [(FRAMES, WIN, CP, CC), (2, C, CC), col_send, col_send],
        [smem] + [vmem] * 4,
        [pltpu.VMEM((FRAMES, CR + 2 * REACH, CP, CC), bf16)],
        cost(1 << 20, 2 << 20),
    )(off, red, recv_a, recv_b, cols)
    recv_a = swap(send_a, "cols", False)
    recv_b = swap(send_b, "cols", True)
    (out,) = call(
        lambda *refs: join_kernel(ncols, *refs),
        [(C * CR, CC)],
        [smem] + [vmem] * 7,
        [
            pltpu.VMEM(((WIN - CR // 2) * KROW + KALL - 3 * KROW, 2 * CC), bf16),
            pltpu.VMEM((C * CR, CC), f32),
        ],
        cost(2 * C * KALL * CR * CC, 4 << 20),
    )(off, win, edge, cur_t, recv_a, recv_b, wall, mixer_bias.reshape(C, 1))
    return out.reshape(C, CR, CC)


def solution(mesh):
    in_specs = (P(None, "rows", "cols"), P(None, None, "rows", "cols"), P(), P(), P(), P())
    out_specs = P(None, "rows", "cols")
    return jax.shard_map(body, mesh=mesh, in_specs=in_specs, out_specs=out_specs, check_vma=False)
```

```python
import jax
import jax.numpy as jnp
from jax import lax
from jax.experimental import pallas as pl
from jax.experimental.pallas import tpu as pltpu
from jax.sharding import PartitionSpec as P

C = 128
CP = 32
FRAMES = 3
CR = 16
CC = 128
SHIFT_X = 16
SHIFT_Y = 8
REACH = SHIFT_Y + 1
WIN = CR + 2
KROW = 3 * C + 3 * FRAMES * CP
KALL = 2048
TILES = 3
SEG = 21
SEG0 = CC - SEG
VMEM_LIMIT = 48 * 1024 * 1024
f32 = jnp.float32
bf16 = jnp.bfloat16


def slots(off, axis):
    pos = [off[axis, k] > 0 for k in range(FRAMES)]
    first_pos = jnp.where(pos[0], 0, jnp.where(pos[1], 1, 2))
    last_pos = jnp.where(pos[2], 2, jnp.where(pos[1], 1, 0))
    first_neg = jnp.where(pos[0], jnp.where(pos[1], 2, 1), 0)
    last_neg = jnp.where(pos[2], jnp.where(pos[1], 0, 1), 2)
    place = [
        jnp.where(pos[k], jnp.where(first_pos == k, 0, 1), jnp.where(first_neg == k, 0, 1))
        for k in range(FRAMES)
    ]
    return pos, (first_pos, last_pos), (first_neg, last_neg), place


def lanes(shape):
    return lax.broadcasted_iota(jnp.int32, shape, len(shape) - 1)


def compress_kernel(
    off_hbm, hist, cur, w_hbm, red, send_a, send_b, off, w, hbuf, cbuf, fbuf, sems
):
    copies = [pltpu.make_async_copy(hist.at[k], hbuf.at[k], sems.at[k]) for k in range(FRAMES)]
    copies.append(pltpu.make_async_copy(cur, cbuf, sems.at[FRAMES]))
    small = [
        pltpu.make_async_copy(w_hbm, w, sems.at[FRAMES + 1]),
        pltpu.make_async_copy(off_hbm, off, sems.at[FRAMES + 2]),
    ]
    for copy in small[:1] + copies + small[1:]:
        copy.start()
    row = lax.axis_index("rows")
    even = row % 2 == 0
    small[0].wait()
    for k in range(FRAMES):
        copies[k].wait()
        fbuf[k] = hbuf[k].astype(f32)
        x = jnp.concatenate(
            [fbuf[k, pl.ds(y, C, stride=CR), :].astype(bf16) for y in range(CR)], axis=1
        )
        r = jnp.dot(w[...], x, preferred_element_type=f32).astype(bf16)
        for y in range(CR):
            red[k, y] = r[:, y * CC : (y + 1) * CC]
    copies[FRAMES].wait()
    fbuf[0] = cbuf[...].astype(f32)
    top = fbuf[0, pl.ds(0, C, stride=CR), :].astype(bf16).reshape(C // CP, CP, CC)
    bottom = fbuf[0, pl.ds(CR - 1, C, stride=CR), :].astype(bf16).reshape(C // CP, CP, CC)
    small[1].wait()
    _, posf, negf, _ = slots(off, 0)
    for send, down in ((send_a, even), (send_b, jnp.logical_not(even))):
        start = jnp.where(down, CR - REACH, 0)
        for s in range(2):
            k = jnp.where(down, posf[s], negf[s])
            for i in range(REACH):
                send[s * REACH + i] = red[k, start + i]
        send[2 * REACH : 2 * REACH + C // CP] = jnp.where(down, bottom, top)


def prepare_kernel(cur, wt, cur_t, cols, wall, fbuf):
    fbuf[...] = cur[...].astype(f32)
    lane = lanes((C, CC))
    first = jnp.zeros((C, CC), f32)
    last = jnp.zeros((C, CC), f32)
    for y in range(CR):
        t = fbuf[pl.ds(y, C, stride=CR), :]
        cur_t[y] = t.astype(bf16)
        first = jnp.where(lane == y + 1, pltpu.roll(t, y + 1, 1), first)
        last = jnp.where(lane == y + 1, pltpu.roll(t, y + 2, 1), last)
    cols[0] = first.astype(bf16)
    cols[1] = last.astype(bf16)
    parts = []
    for i in range(3):
        parts += [wt[i, j, :C, :] for j in range(3)]
        parts += [wt[i, j, C:, :] for j in range(3)]
    parts.append(jnp.zeros((KALL - 3 * KROW, C), bf16))
    tall = jnp.concatenate(parts, axis=0).astype(f32)
    for b in range(KALL // C):
        wall[:, b * C : (b + 1) * C] = tall[b * C : (b + 1) * C].T.astype(bf16)


def window_kernel(nrows, off, red, recv_a, recv_b, cols, win, edge, send_a, send_b, cb):
    row = lax.axis_index("rows")
    col = lax.axis_index("cols")
    even = row % 2 == 0
    has_above = row > 0
    has_below = row < nrows - 1
    pos, _, _, place = slots(off, 0)
    zero = jnp.zeros((REACH, CP, CC), bf16)
    for k in range(FRAMES):
        cb[k, REACH : REACH + CR] = red[k]
        at = pl.ds(place[k] * REACH, REACH)
        from_a = recv_a[at]
        from_b = recv_b[at]
        use_a = jnp.logical_xor(pos[k], even)
        ok = jnp.where(pos[k], has_above, has_below)
        halo = jnp.where(ok, jnp.where(use_a, from_a, from_b), zero)
        cb[k, pl.ds(jnp.where(pos[k], 0, REACH + CR), REACH)] = halo
    for k in range(FRAMES):
        start = SHIFT_Y - off[0, k]
        for r in range(WIN):
            v = cb[k, start + r]
            if r == 0:
                v = jnp.where(has_above, v, jnp.zeros_like(v))
            if r == WIN - 1:
                v = jnp.where(has_below, v, jnp.zeros_like(v))
            win[k, r] = v
    tail_a = recv_a[2 * REACH : 2 * REACH + C // CP].reshape(C, CC)
    tail_b = recv_b[2 * REACH : 2 * REACH + C // CP].reshape(C, CC)
    blank = jnp.zeros((C, CC), bf16)
    above = jnp.where(has_above, jnp.where(even, tail_b, tail_a), blank)
    below = jnp.where(has_below, jnp.where(even, tail_a, tail_b), blank)
    edge[0] = above
    edge[1] = below
    above = above.astype(f32)
    below = below.astype(f32)
    ceven = col % 2 == 0
    _, posf, negf, _ = slots(off, 1)
    lane = lanes((CP, CC))
    wide = lanes((C, CC))
    first = jnp.where(wide == 0, above, cols[0].astype(f32))
    first = jnp.where(wide == WIN - 1, pltpu.roll(below, WIN - 1, 1), first)
    last = jnp.where(wide == 0, pltpu.roll(above, 1, 1), cols[1].astype(f32))
    last = jnp.where(wide == WIN - 1, pltpu.roll(below, WIN, 1), last)
    for send, right in ((send_a, ceven), (send_b, jnp.logical_not(ceven))):
        back = jnp.where(right, SEG0, 0)
        for s in range(2):
            k = jnp.where(right, posf[s], negf[s])
            for t in range(TILES):
                total = jnp.zeros((CP, CC), f32)
                for q in range(WIN // TILES):
                    piece = win[k, t + TILES * q].astype(f32)
                    piece = pltpu.roll(piece, (SEG * q - back + CC) % CC, 1)
                    total = jnp.where((lane >= SEG * q) & (lane < SEG * (q + 1)), piece, total)
                send[s * TILES + t] = total.astype(bf16)
        pack = jnp.where(right, last, first)
        total = pack[:CP]
        for g in range(1, C // CP):
            total = jnp.where(lane >= CP * g, pltpu.roll(pack[CP * g : CP * (g + 1)], CP * g, 1), total)
        send[2 * TILES] = total.astype(bf16)


def join_kernel(ncols, off, win, edge, cur_t, recv_a, recv_b, wall, bias, out, x2, acc):
    col = lax.axis_index("cols")
    ceven = col % 2 == 0
    has_left = col > 0
    has_right = col < ncols - 1
    pos, _, _, place = slots(off, 1)
    lane = lanes((CP, CC))
    wide = lanes((C, CC))

    def unpack(ref):
        t = ref[2 * TILES].astype(f32)
        return jnp.concatenate(
            [t] + [pltpu.roll(t, CC - CP * g, 1) for g in range(1, C // CP)], axis=0
        )

    pack_a = unpack(recv_a)
    pack_b = unpack(recv_b)
    left = jnp.where(ceven, pack_b, pack_a)
    right = jnp.where(ceven, pack_a, pack_b)
    left = jnp.where(has_left, left, jnp.zeros_like(left))
    right = jnp.where(has_right, right, jnp.zeros_like(right))

    def put(r, at, size, value):
        if r <= WIN - CR // 2 - 1:
            x2[r * KROW + at : r * KROW + at + size, :CC] = value
        if r >= CR // 2:
            q = r - CR // 2
            x2[q * KROW + at : q * KROW + at + size, CC:] = value

    for r in range(WIN):
        if r == 0:
            here = edge[0]
        elif r == WIN - 1:
            here = edge[1]
        else:
            here = cur_t[r - 1]
        put(r, C, C, here)
        here = here.astype(f32)
        before = jnp.where(wide == 0, pltpu.roll(left, (CC - r) % CC, 1), pltpu.roll(here, 1, 1))
        after = jnp.where(
            wide == CC - 1, pltpu.roll(right, CC - 1 - r, 1), pltpu.roll(here, CC - 1, 1)
        )
        put(r, 0, C, before.astype(bf16))
        put(r, 2 * C, C, after.astype(bf16))
    for k in range(FRAMES):
        use_a = jnp.logical_xor(pos[k], ceven)
        ok = jnp.where(pos[k], has_left, has_right)
        back = jnp.where(pos[k], SEG0, 0)
        tiles = []
        for t in range(TILES):
            a = recv_a[place[k] * TILES + t].astype(f32)
            b = recv_b[place[k] * TILES + t].astype(f32)
            v = jnp.where(use_a, a, b)
            tiles.append(jnp.where(ok, v, jnp.zeros_like(v)))
        taps = []
        for j in range(3):
            s = off[1, k] + 1 - j
            lo = jnp.where(pos[k], CC - s, 0)
            hi = jnp.where(pos[k], CC, -s)
            mask = (lane >= lo) & (lane < hi)
            outside = None
            if j == 0:
                outside = jnp.logical_and(lane == 0, jnp.logical_not(has_left))
            if j == 2:
                outside = jnp.logical_and(lane == CC - 1, jnp.logical_not(has_right))
            taps.append(((s + CC) % CC, mask, outside))
        for r in range(WIN):
            t, q = r % TILES, r // TILES
            local = win[k, r].astype(f32)
            halo = pltpu.roll(tiles[t], (back - SEG * q + CC) % CC, 1)
            for j in range(3):
                s, mask, outside = taps[j]
                v = pltpu.roll(jnp.where(mask, halo, local), s, 1)
                if outside is not None:
                    v = jnp.where(outside, jnp.zeros_like(v), v)
                put(r, 3 * C + j * FRAMES * CP + k * CP, CP, v.astype(bf16))
    x2[(WIN - CR // 2) * KROW :, :] = jnp.zeros((KALL - 3 * KROW, 2 * CC), bf16)
    bias_col = jnp.broadcast_to(bias[...], (C, 2 * CC))
    for y in range(CR // 2):
        p = jnp.dot(
            wall[...], x2[y * KROW : y * KROW + KALL, :], preferred_element_type=f32
        )
        p = jnp.maximum(p + bias_col, 0.0)
        acc[pl.ds(y, C, stride=CR), :] = p[:, :CC]
        acc[pl.ds(y + CR // 2, C, stride=CR), :] = p[:, CC:]
    out[...] = acc[...].astype(bf16)


def swap(x, axis, shifted):
    size = lax.axis_size(axis)
    if shifted:
        pairs = [(i, (i - 1 if i % 2 == 0 else i + 1) % size) for i in range(size)]
    else:
        pairs = [(i, i ^ 1) for i in range(size)]
    return lax.ppermute(x, axis, pairs)


def cost(flops, bytes_accessed):
    return pl.CostEstimate(flops=flops, bytes_accessed=bytes_accessed, transcendentals=0)


def call(kernel, outs, specs, scratch, estimate):
    vmem = pl.BlockSpec(memory_space=pltpu.VMEM)
    return pl.pallas_call(
        kernel,
        out_shape=[jax.ShapeDtypeStruct(shape, bf16) for shape in outs],
        in_specs=specs,
        out_specs=[vmem] * len(outs),
        scratch_shapes=scratch,
        cost_estimate=estimate,
        compiler_params=pltpu.CompilerParams(vmem_limit_bytes=VMEM_LIMIT),
    )


def body(current_frame, history_frames, offsets, compress_weight, mixer_weight, mixer_bias):
    smem = pl.BlockSpec(memory_space=pltpu.SMEM)
    vmem = pl.BlockSpec(memory_space=pltpu.VMEM)
    hbm = pl.BlockSpec(memory_space=pltpu.HBM)
    off = offsets.T
    hist = history_frames.reshape(FRAMES, C * CR, CC)
    cur = current_frame.reshape(C * CR, CC)
    wt = mixer_weight.transpose(0, 1, 3, 2)
    nrows, ncols = lax.axis_size("rows"), lax.axis_size("cols")
    row_send = (2 * REACH + C // CP, CP, CC)
    col_send = (2 * TILES + 1, CP, CC)
    red, send_a, send_b = call(
        compress_kernel,
        [(FRAMES, CR, CP, CC), row_send, row_send],
        [hbm] * 4,
        [
            pltpu.SMEM((2, FRAMES), jnp.int32),
            pltpu.VMEM((CP, C), bf16),
            pltpu.VMEM((FRAMES, C * CR, CC), bf16),
            pltpu.VMEM((C * CR, CC), bf16),
            pltpu.VMEM((FRAMES, C * CR, CC), f32),
            pltpu.SemaphoreType.DMA((FRAMES + 3,)),
        ],
        cost(2 * FRAMES * CP * C * CR * CC, 3 << 20),
    )(*[pltpu.with_memory_space_constraint(v, pltpu.HBM) for v in (off, hist, cur, compress_weight)])
    recv_a = swap(send_a, "rows", False)
    recv_b = swap(send_b, "rows", True)
    cur_t, cols, wall = call(
        prepare_kernel,
        [(CR, C, CC), (2, C, CC), (C, KALL)],
        [vmem, vmem],
        [pltpu.VMEM((C * CR, CC), f32)],
        cost(1 << 20, 3 << 20),
    )(cur, wt)
    win, edge, send_a, send_b = call(
        lambda *refs: window_kernel(nrows, *refs),
        [(FRAMES, WIN, CP, CC), (2, C, CC), col_send, col_send],
        [smem] + [vmem] * 4,
        [pltpu.VMEM((FRAMES, CR + 2 * REACH, CP, CC), bf16)],
        cost(1 << 20, 2 << 20),
    )(off, red, recv_a, recv_b, cols)
    recv_a = swap(send_a, "cols", False)
    recv_b = swap(send_b, "cols", True)
    (out,) = call(
        lambda *refs: join_kernel(ncols, *refs),
        [(C * CR, CC)],
        [smem] + [vmem] * 7,
        [
            pltpu.VMEM(((WIN - CR // 2) * KROW + KALL - 3 * KROW, 2 * CC), bf16),
            pltpu.VMEM((C * CR, CC), f32),
        ],
        cost(2 * C * KALL * CR * CC, 4 << 20),
    )(off, win, edge, cur_t, recv_a, recv_b, wall, mixer_bias.reshape(C, 1))
    return out.reshape(C, CR, CC)


def solution(mesh):
    in_specs = (P(None, "rows", "cols"), P(None, None, "rows", "cols"), P(), P(), P(), P())
    out_specs = P(None, "rows", "cols")
    return jax.shard_map(body, mesh=mesh, in_specs=in_specs, out_specs=out_specs, check_vma=False)
```

```python
import jax
import jax.numpy as jnp
from jax import lax
from jax.experimental import pallas as pl
from jax.experimental.pallas import tpu as pltpu
from jax.sharding import PartitionSpec as P

C = 128
CP = 32
FRAMES = 3
CR = 16
CC = 128
SHIFT_X = 16
SHIFT_Y = 8
REACH = SHIFT_Y + 1
WIN = CR + 2
KROW = 3 * C + 3 * FRAMES * CP
KALL = 2048
EROW = 2 * C + 3 * FRAMES * CP
KEDGE = 1664
TILES = 3
SEG = 21
SEG0 = CC - SEG
VMEM_LIMIT = 48 * 1024 * 1024
f32 = jnp.float32
bf16 = jnp.bfloat16


def slots(off, axis):
    pos = [off[axis, k] > 0 for k in range(FRAMES)]
    first_pos = jnp.where(pos[0], 0, jnp.where(pos[1], 1, 2))
    last_pos = jnp.where(pos[2], 2, jnp.where(pos[1], 1, 0))
    first_neg = jnp.where(pos[0], jnp.where(pos[1], 2, 1), 0)
    last_neg = jnp.where(pos[2], jnp.where(pos[1], 0, 1), 2)
    place = [
        jnp.where(pos[k], jnp.where(first_pos == k, 0, 1), jnp.where(first_neg == k, 0, 1))
        for k in range(FRAMES)
    ]
    return pos, (first_pos, last_pos), (first_neg, last_neg), place


def lanes(shape):
    return lax.broadcasted_iota(jnp.int32, shape, len(shape) - 1)


def compress_kernel(
    off_hbm, hist, cur, w_hbm, red, send_a, send_b, off, w, hbuf, cbuf, fbuf, sems
):
    copies = [pltpu.make_async_copy(hist.at[k], hbuf.at[k], sems.at[k]) for k in range(FRAMES)]
    copies.append(pltpu.make_async_copy(cur, cbuf, sems.at[FRAMES]))
    small = [
        pltpu.make_async_copy(w_hbm, w, sems.at[FRAMES + 1]),
        pltpu.make_async_copy(off_hbm, off, sems.at[FRAMES + 2]),
    ]
    for copy in small[:1] + copies + small[1:]:
        copy.start()
    row = lax.axis_index("rows")
    even = row % 2 == 0
    small[0].wait()
    for k in range(FRAMES):
        copies[k].wait()
        fbuf[k] = hbuf[k].astype(f32)
        x = jnp.concatenate(
            [fbuf[k, pl.ds(y, C, stride=CR), :].astype(bf16) for y in range(CR)], axis=1
        )
        r = jnp.dot(w[...], x, preferred_element_type=f32).astype(bf16)
        for y in range(CR):
            red[k, y] = r[:, y * CC : (y + 1) * CC]
    copies[FRAMES].wait()
    fbuf[0] = cbuf[...].astype(f32)
    top = fbuf[0, pl.ds(0, C, stride=CR), :].astype(bf16).reshape(C // CP, CP, CC)
    bottom = fbuf[0, pl.ds(CR - 1, C, stride=CR), :].astype(bf16).reshape(C // CP, CP, CC)
    small[1].wait()
    _, posf, negf, _ = slots(off, 0)
    for send, down in ((send_a, even), (send_b, jnp.logical_not(even))):
        start = jnp.where(down, CR - REACH, 0)
        for s in range(2):
            k = jnp.where(down, posf[s], negf[s])
            for i in range(REACH):
                send[s * REACH + i] = red[k, start + i]
        send[2 * REACH : 2 * REACH + C // CP] = jnp.where(down, bottom, top)


def spot(r):
    return SEG * (r // TILES) + r % TILES


def segment_lane(shape):
    lane = lanes(shape)
    base = jnp.zeros(shape, jnp.int32)
    for m in range(1, CC // SEG + 1):
        base = jnp.where(lane >= SEG * m, SEG * m, base)
    return lane - base


def prepare_kernel(cur, wt, cur_t, cols, wall, wedge, fbuf):
    fbuf[...] = cur[...].astype(f32)
    lane = lanes((C, CC))
    first = jnp.zeros((C, CC), f32)
    last = jnp.zeros((C, CC), f32)
    for y in range(CR):
        t = fbuf[pl.ds(y, C, stride=CR), :]
        cur_t[y] = t.astype(bf16)
        at = spot(y + 1)
        first = jnp.where(lane == at, pltpu.roll(t, at, 1), first)
        last = jnp.where(lane == at, pltpu.roll(t, at + 1, 1), last)
    cols[0] = first.astype(bf16)
    cols[1] = last.astype(bf16)
    for dest, taps, size in ((wall, (0, 1, 2), KALL), (wedge, (0, 2), KEDGE)):
        parts = []
        for i in range(3):
            parts += [wt[i, j, :C, :] for j in taps]
            parts += [wt[i, j, C:, :] for j in range(3)]
        parts.append(jnp.zeros((size - sum(p.shape[0] for p in parts), C), bf16))
        tall = jnp.concatenate(parts, axis=0).astype(f32)
        for b in range(size // C):
            dest[:, b * C : (b + 1) * C] = tall[b * C : (b + 1) * C].T.astype(bf16)


def row_halo(nrows, off, red, recv_a, recv_b, cb):
    row = lax.axis_index("rows")
    even = row % 2 == 0
    has_above = row > 0
    has_below = row < nrows - 1
    pos, _, _, place = slots(off, 0)
    zero = jnp.zeros((REACH, CP, CC), bf16)
    for k in range(FRAMES):
        cb[k, REACH : REACH + CR] = red[k]
        at = pl.ds(place[k] * REACH, REACH)
        from_a = recv_a[at]
        from_b = recv_b[at]
        use_a = jnp.logical_xor(pos[k], even)
        ok = jnp.where(pos[k], has_above, has_below)
        halo = jnp.where(ok, jnp.where(use_a, from_a, from_b), zero)
        cb[k, pl.ds(jnp.where(pos[k], 0, REACH + CR), REACH)] = halo
    tail_a = recv_a[2 * REACH : 2 * REACH + C // CP].reshape(C, CC)
    tail_b = recv_b[2 * REACH : 2 * REACH + C // CP].reshape(C, CC)
    blank = jnp.zeros((C, CC), bf16)
    above = jnp.where(has_above, jnp.where(even, tail_b, tail_a), blank)
    below = jnp.where(has_below, jnp.where(even, tail_a, tail_b), blank)
    return above, below, has_above, has_below


def window_row(off, cb, k, r, has_above, has_below):
    v = cb[k, SHIFT_Y - off[0, k] + r]
    if r == 0:
        v = jnp.where(has_above, v, jnp.zeros_like(v))
    if r == WIN - 1:
        v = jnp.where(has_below, v, jnp.zeros_like(v))
    return v


def pack_kernel(nrows, off, red, recv_a, recv_b, cols, send_a, send_b, cb):
    above, below, has_above, has_below = row_halo(nrows, off, red, recv_a, recv_b, cb)
    above = above.astype(f32)
    below = below.astype(f32)
    ceven = lax.axis_index("cols") % 2 == 0
    _, posf, negf, _ = slots(off, 1)
    lane = lanes((CP, CC))
    inner = segment_lane((CP, CC))
    wide = lanes((C, CC))
    end = spot(WIN - 1)
    first = jnp.where(wide == 0, above, cols[0].astype(f32))
    first = jnp.where(wide == end, pltpu.roll(below, end, 1), first)
    last = jnp.where(wide == 0, pltpu.roll(above, 1, 1), cols[1].astype(f32))
    last = jnp.where(wide == end, pltpu.roll(below, end + 1, 1), last)
    for send, right in ((send_a, ceven), (send_b, jnp.logical_not(ceven))):
        back = jnp.where(right, SEG0, 0)
        for s in range(2):
            k = jnp.where(right, posf[s], negf[s])
            for t in range(TILES):
                total = jnp.zeros((CP, CC), f32)
                for q in range(WIN // TILES):
                    piece = window_row(off, cb, k, t + TILES * q, has_above, has_below)
                    piece = pltpu.roll(piece.astype(f32), (SEG * q - back + CC) % CC, 1)
                    total = piece if q == 0 else jnp.where(lane >= SEG * q, piece, total)
                send[s * TILES + t] = total.astype(bf16)
        pack = jnp.where(right, last, first)
        total = pack[:CP]
        for g in range(1, C // CP):
            moved = pltpu.roll(pack[CP * g : CP * (g + 1)], TILES * g, 1)
            total = jnp.where(inner >= TILES * g, moved, total)
        send[2 * TILES] = total.astype(bf16)


def local_kernel(nrows, ncols, off, red, recv_a, recv_b, cur_t, wall, bias, part, cb, x2):
    above, below, has_above, has_below = row_halo(nrows, off, red, recv_a, recv_b, cb)
    col = lax.axis_index("cols")
    has_left = col > 0
    has_right = col < ncols - 1
    pos, _, _, _ = slots(off, 1)
    lane = lanes((CP, CC))
    wide = lanes((C, CC))

    def put(r, at, size, value):
        if r <= WIN - CR // 2 - 1:
            x2[r * KROW + at : r * KROW + at + size, :CC] = value
        if r >= CR // 2:
            q = r - CR // 2
            x2[q * KROW + at : q * KROW + at + size, CC:] = value

    taps = []
    for k in range(FRAMES):
        for j in range(3):
            s = off[1, k] + 1 - j
            lo = jnp.where(pos[k], s, 0)
            hi = jnp.where(pos[k], CC, CC + s)
            if j == 0:
                lo = jnp.where(has_left, lo, jnp.maximum(lo, 1))
            if j == 2:
                hi = jnp.where(has_right, hi, jnp.minimum(hi, CC - 1))
            taps.append(((s + CC) % CC, (lane >= lo) & (lane < hi)))
    for r in range(WIN):
        here = above if r == 0 else below if r == WIN - 1 else cur_t[r - 1]
        put(r, C, C, here)
        here = here.astype(f32)
        zero = jnp.zeros_like(here)
        put(r, 0, C, jnp.where(wide == 0, zero, pltpu.roll(here, 1, 1)).astype(bf16))
        put(r, 2 * C, C, jnp.where(wide == CC - 1, zero, pltpu.roll(here, CC - 1, 1)).astype(bf16))
        for k in range(FRAMES):
            own = window_row(off, cb, k, r, has_above, has_below).astype(f32)
            for j in range(3):
                s, mask = taps[3 * k + j]
                v = jnp.where(mask, pltpu.roll(own, s, 1), jnp.zeros_like(own))
                put(r, 3 * C + j * FRAMES * CP + k * CP, CP, v.astype(bf16))
    x2[(WIN - CR // 2) * KROW :, :] = jnp.zeros((KALL - 3 * KROW, 2 * CC), bf16)
    bias_col = jnp.broadcast_to(bias[...], (C, 2 * CC))
    for y in range(CR // 2):
        p = jnp.dot(
            wall[...], x2[y * KROW : y * KROW + KALL, :], preferred_element_type=f32
        )
        part[y] = p + bias_col


def finish_kernel(ncols, off, recv_a, recv_b, part, wedge, out, xx, acc):
    col = lax.axis_index("cols")
    ceven = col % 2 == 0
    has_left = col > 0
    has_right = col < ncols - 1
    pos, _, _, place = slots(off, 1)
    inner = segment_lane((CP, CC))
    zero = jnp.zeros((CP, CC), bf16)
    cur_a = recv_a[2 * TILES].astype(f32)
    cur_b = recv_b[2 * TILES].astype(f32)
    left = jnp.where(ceven, cur_b, cur_a)
    right = jnp.where(ceven, cur_a, cur_b)
    left = jnp.where(has_left, left, jnp.zeros_like(left))
    right = jnp.where(has_right, right, jnp.zeros_like(right))
    frames = []
    for k in range(FRAMES):
        use_a = jnp.logical_xor(pos[k], ceven)
        ok = jnp.where(pos[k], has_left, has_right)
        tiles = []
        for t in range(TILES):
            v = jnp.where(use_a, recv_a[place[k] * TILES + t], recv_b[place[k] * TILES + t])
            tiles.append(jnp.where(ok, v, zero).astype(f32))
        masks = []
        for j in range(3):
            s = off[1, k] + 1 - j
            lo = jnp.where(pos[k], 0, SEG + s)
            hi = jnp.where(pos[k], s, SEG)
            mask = (inner >= lo) & (inner < hi)
            masks.append((jnp.where(pos[k], s - SEG, s + SEG), mask))
        frames.append((tiles, masks))
    for u in range(TILES + 2):
        base = u * EROW
        back = SEG * (u // TILES)
        shift = back + u % TILES
        for g in range(C // CP):
            rows = slice(base + g * CP, base + (g + 1) * CP)
            v = pltpu.roll(left, (2 * CC - shift - TILES * g) % CC, 1)
            xx[rows, :CC] = jnp.where(inner == 0, v, 0.0).astype(bf16)
            xx[rows, CC:] = zero
            rows = slice(base + C + g * CP, base + C + (g + 1) * CP)
            v = pltpu.roll(right, (2 * CC + SEG - 1 - shift - TILES * g) % CC, 1)
            xx[rows, :CC] = zero
            xx[rows, CC:] = jnp.where(inner == SEG - 1, v, 0.0).astype(bf16)
        for k in range(FRAMES):
            tiles, masks = frames[k]
            for j in range(3):
                move, mask = masks[j]
                v = pltpu.roll(tiles[u % TILES], (move - back + 2 * CC) % CC, 1)
                v = jnp.where(mask, v, 0.0).astype(bf16)
                at = base + 2 * C + j * FRAMES * CP + k * CP
                xx[at : at + CP, :CC] = jnp.where(pos[k], v, zero)
                xx[at : at + CP, CC:] = jnp.where(pos[k], zero, v)
    xx[(TILES + 2) * EROW :, :] = jnp.zeros((KEDGE - 3 * EROW, 2 * CC), bf16)
    wide = lanes((C, CC))
    for t in range(TILES):
        p = jnp.dot(
            wedge[...], xx[t * EROW : t * EROW + KEDGE, :], preferred_element_type=f32
        )
        for y in range(t, CR, TILES):
            q = y // TILES
            lft = pltpu.roll(p[:, :CC], (CC - SEG * q) % CC, 1)
            rgt = pltpu.roll(p[:, CC:], (SEG0 - SEG * q) % CC, 1)
            v = jnp.where(wide < SEG, lft, jnp.where(wide >= SEG0, rgt, 0.0))
            at = 0 if y < CR // 2 else CC
            v = jnp.maximum(part[y % (CR // 2), :, at : at + CC] + v, 0.0)
            acc[pl.ds(y, C, stride=CR), :] = v
    out[...] = acc[...].astype(bf16)


def swap(x, axis, shifted):
    size = lax.axis_size(axis)
    if shifted:
        pairs = [(i, (i - 1 if i % 2 == 0 else i + 1) % size) for i in range(size)]
    else:
        pairs = [(i, i ^ 1) for i in range(size)]
    return lax.ppermute(x, axis, pairs)


def cost(flops, bytes_accessed):
    return pl.CostEstimate(flops=flops, bytes_accessed=bytes_accessed, transcendentals=0)


def call(kernel, outs, specs, scratch, estimate):
    vmem = pl.BlockSpec(memory_space=pltpu.VMEM)
    return pl.pallas_call(
        kernel,
        out_shape=[jax.ShapeDtypeStruct(*out) for out in outs],
        in_specs=specs,
        out_specs=[vmem] * len(outs),
        scratch_shapes=scratch,
        cost_estimate=estimate,
        compiler_params=pltpu.CompilerParams(vmem_limit_bytes=VMEM_LIMIT),
    )


def body(current_frame, history_frames, offsets, compress_weight, mixer_weight, mixer_bias):
    smem = pl.BlockSpec(memory_space=pltpu.SMEM)
    vmem = pl.BlockSpec(memory_space=pltpu.VMEM)
    hbm = pl.BlockSpec(memory_space=pltpu.HBM)
    off = offsets.T
    hist = history_frames.reshape(FRAMES, C * CR, CC)
    cur = current_frame.reshape(C * CR, CC)
    wt = mixer_weight.transpose(0, 1, 3, 2)
    nrows, ncols = lax.axis_size("rows"), lax.axis_size("cols")
    row_send = (2 * REACH + C // CP, CP, CC)
    col_send = (2 * TILES + 1, CP, CC)
    red, send_a, send_b = call(
        compress_kernel,
        [((FRAMES, CR, CP, CC), bf16), (row_send, bf16), (row_send, bf16)],
        [hbm] * 4,
        [
            pltpu.SMEM((2, FRAMES), jnp.int32),
            pltpu.VMEM((CP, C), bf16),
            pltpu.VMEM((FRAMES, C * CR, CC), bf16),
            pltpu.VMEM((C * CR, CC), bf16),
            pltpu.VMEM((FRAMES, C * CR, CC), f32),
            pltpu.SemaphoreType.DMA((FRAMES + 3,)),
        ],
        cost(2 * FRAMES * CP * C * CR * CC, 3 << 20),
    )(*[pltpu.with_memory_space_constraint(v, pltpu.HBM) for v in (off, hist, cur, compress_weight)])
    recv_a = swap(send_a, "rows", False)
    recv_b = swap(send_b, "rows", True)
    cur_t, cols, wall, wedge = call(
        prepare_kernel,
        [((CR, C, CC), bf16), ((2, C, CC), bf16), ((C, KALL), bf16), ((C, KEDGE), bf16)],
        [vmem, vmem],
        [pltpu.VMEM((C * CR, CC), f32)],
        cost(1 << 20, 3 << 20),
    )(cur, wt)
    halo_rows = pltpu.VMEM((FRAMES, CR + 2 * REACH, CP, CC), bf16)
    csend_a, csend_b = call(
        lambda *refs: pack_kernel(nrows, *refs),
        [(col_send, bf16), (col_send, bf16)],
        [smem] + [vmem] * 4,
        [halo_rows],
        cost(1 << 20, 2 << 20),
    )(off, red, recv_a, recv_b, cols)
    crecv_a = swap(csend_a, "cols", False)
    crecv_b = swap(csend_b, "cols", True)
    (part,) = call(
        lambda *refs: local_kernel(nrows, ncols, *refs),
        [((CR // 2, C, 2 * CC), f32)],
        [smem] + [vmem] * 6,
        [halo_rows, pltpu.VMEM(((WIN - CR // 2) * KROW + KALL - 3 * KROW, 2 * CC), bf16)],
        cost(2 * C * KALL * CR * CC, 4 << 20),
    )(off, red, recv_a, recv_b, cur_t, wall, mixer_bias.reshape(C, 1))
    (out,) = call(
        lambda *refs: finish_kernel(ncols, *refs),
        [((C * CR, CC), bf16)],
        [smem] + [vmem] * 4,
        [
            pltpu.VMEM(((TILES + 2) * EROW + KEDGE - 3 * EROW, 2 * CC), bf16),
            pltpu.VMEM((C * CR, CC), f32),
        ],
        cost(1 << 20, 2 << 20),
    )(off, crecv_a, crecv_b, part, wedge)
    return out.reshape(C, CR, CC)


def solution(mesh):
    in_specs = (P(None, "rows", "cols"), P(None, None, "rows", "cols"), P(), P(), P(), P())
    out_specs = P(None, "rows", "cols")
    return jax.shard_map(body, mesh=mesh, in_specs=in_specs, out_specs=out_specs, check_vma=False)
```

```python
import jax
import jax.numpy as jnp
from jax import lax
from jax.experimental import pallas as pl
from jax.experimental.pallas import tpu as pltpu
from jax.sharding import PartitionSpec as P

C = 128
CP = 32
FRAMES = 3
CR = 16
CC = 128
SHIFT_X = 16
SHIFT_Y = 8
REACH = SHIFT_Y + 1
WIN = CR + 2
KROW = 3 * C + 3 * FRAMES * CP
KALL = 2048
EROW = 2 * C + 3 * FRAMES * CP
KEDGE = 1664
TILES = 3
SEG = 21
SEG0 = CC - SEG
VMEM_LIMIT = 48 * 1024 * 1024
f32 = jnp.float32
bf16 = jnp.bfloat16


def slots(off, axis):
    pos = [off[axis][k] > 0 for k in range(FRAMES)]
    first_pos = jnp.where(pos[0], 0, jnp.where(pos[1], 1, 2))
    last_pos = jnp.where(pos[2], 2, jnp.where(pos[1], 1, 0))
    first_neg = jnp.where(pos[0], jnp.where(pos[1], 2, 1), 0)
    last_neg = jnp.where(pos[2], jnp.where(pos[1], 0, 1), 2)
    place = [
        jnp.where(pos[k], jnp.where(first_pos == k, 0, 1), jnp.where(first_neg == k, 0, 1))
        for k in range(FRAMES)
    ]
    return pos, (first_pos, last_pos), (first_neg, last_neg), place


def scalars(ref):
    return [[ref[axis, k] for k in range(FRAMES)] for axis in range(2)]


def pick(values, k):
    return jnp.where(k == 0, values[0], jnp.where(k == 1, values[1], values[2]))


def lanes(shape):
    return lax.broadcasted_iota(jnp.int32, shape, len(shape) - 1)


def compress_kernel(
    off_hbm, hist, cur, w_hbm, red, send_a, send_b, off, w, hbuf, cbuf, fbuf, sems
):
    copies = [pltpu.make_async_copy(hist.at[k], hbuf.at[k], sems.at[k]) for k in range(FRAMES)]
    copies.append(pltpu.make_async_copy(cur, cbuf, sems.at[FRAMES]))
    small = [
        pltpu.make_async_copy(w_hbm, w, sems.at[FRAMES + 1]),
        pltpu.make_async_copy(off_hbm, off, sems.at[FRAMES + 2]),
    ]
    for copy in small[:1] + copies + small[1:]:
        copy.start()
    row = lax.axis_index("rows")
    even = row % 2 == 0
    small[0].wait()
    for k in range(FRAMES):
        copies[k].wait()
        fbuf[k] = hbuf[k].astype(f32)
        x = jnp.concatenate(
            [fbuf[k, pl.ds(y, C, stride=CR), :].astype(bf16) for y in range(CR)], axis=1
        )
        r = jnp.dot(w[...], x, preferred_element_type=f32).astype(bf16)
        for y in range(CR):
            red[k, y] = r[:, y * CC : (y + 1) * CC]
    copies[FRAMES].wait()
    fbuf[0] = cbuf[...].astype(f32)
    top = fbuf[0, pl.ds(0, C, stride=CR), :].astype(bf16).reshape(C // CP, CP, CC)
    bottom = fbuf[0, pl.ds(CR - 1, C, stride=CR), :].astype(bf16).reshape(C // CP, CP, CC)
    small[1].wait()
    _, posf, negf, _ = slots(scalars(off), 0)
    for send, down in ((send_a, even), (send_b, jnp.logical_not(even))):
        start = jnp.where(down, CR - REACH, 0)
        for s in range(2):
            k = jnp.where(down, posf[s], negf[s])
            for i in range(REACH):
                send[s * REACH + i] = red[k, start + i]
        send[2 * REACH : 2 * REACH + C // CP] = jnp.where(down, bottom, top)


def spot(r):
    return SEG * (r // TILES) + r % TILES


def segment_lane(shape):
    lane = lanes(shape)
    base = jnp.zeros(shape, jnp.int32)
    for m in range(1, CC // SEG + 1):
        base = jnp.where(lane >= SEG * m, SEG * m, base)
    return lane - base


def prepare_kernel(cur, wt, cur_t, cols, wall, wedge, fbuf):
    fbuf[...] = cur[...].astype(f32)
    lane = lanes((C, CC))
    first = jnp.zeros((C, CC), f32)
    last = jnp.zeros((C, CC), f32)
    for y in range(CR):
        t = fbuf[pl.ds(y, C, stride=CR), :]
        cur_t[y] = t.astype(bf16)
        at = spot(y + 1)
        first = jnp.where(lane == at, pltpu.roll(t, at, 1), first)
        last = jnp.where(lane == at, pltpu.roll(t, at + 1, 1), last)
    cols[0] = first.astype(bf16)
    cols[1] = last.astype(bf16)
    for dest, taps, size in ((wall, (0, 1, 2), KALL), (wedge, (0, 2), KEDGE)):
        parts = []
        for i in range(3):
            parts += [wt[i, j, :C, :] for j in taps]
            parts += [wt[i, j, C:, :] for j in range(3)]
        parts.append(jnp.zeros((size - sum(p.shape[0] for p in parts), C), bf16))
        tall = jnp.concatenate(parts, axis=0).astype(f32)
        for b in range(size // C):
            dest[:, b * C : (b + 1) * C] = tall[b * C : (b + 1) * C].T.astype(bf16)


def row_halo(nrows, off, red, recv_a, recv_b, cb):
    row = lax.axis_index("rows")
    even = row % 2 == 0
    has_above = row > 0
    has_below = row < nrows - 1
    pos, _, _, place = slots(off, 0)
    zero = jnp.zeros((REACH, CP, CC), bf16)
    for k in range(FRAMES):
        cb[k, REACH : REACH + CR] = red[k]
        at = pl.ds(place[k] * REACH, REACH)
        from_a = recv_a[at]
        from_b = recv_b[at]
        use_a = jnp.logical_xor(pos[k], even)
        ok = jnp.where(pos[k], has_above, has_below)
        halo = jnp.where(ok, jnp.where(use_a, from_a, from_b), zero)
        cb[k, pl.ds(jnp.where(pos[k], 0, REACH + CR), REACH)] = halo
    tail_a = recv_a[2 * REACH : 2 * REACH + C // CP].reshape(C, CC)
    tail_b = recv_b[2 * REACH : 2 * REACH + C // CP].reshape(C, CC)
    blank = jnp.zeros((C, CC), bf16)
    above = jnp.where(has_above, jnp.where(even, tail_b, tail_a), blank)
    below = jnp.where(has_below, jnp.where(even, tail_a, tail_b), blank)
    return above, below, has_above, has_below


def window_row(dy, cb, k, r, has_above, has_below):
    v = cb[k, SHIFT_Y - dy + r]
    if r == 0:
        v = jnp.where(has_above, v, jnp.zeros_like(v))
    if r == WIN - 1:
        v = jnp.where(has_below, v, jnp.zeros_like(v))
    return v


def pack_kernel(nrows, off, red, recv_a, recv_b, cols, send_a, send_b, cb):
    off = scalars(off)
    above, below, has_above, has_below = row_halo(nrows, off, red, recv_a, recv_b, cb)
    above = above.astype(f32)
    below = below.astype(f32)
    ceven = lax.axis_index("cols") % 2 == 0
    _, posf, negf, _ = slots(off, 1)
    lane = lanes((CP, CC))
    inner = segment_lane((CP, CC))
    wide = lanes((C, CC))
    end = spot(WIN - 1)
    first = jnp.where(wide == 0, above, cols[0].astype(f32))
    first = jnp.where(wide == end, pltpu.roll(below, end, 1), first)
    last = jnp.where(wide == 0, pltpu.roll(above, 1, 1), cols[1].astype(f32))
    last = jnp.where(wide == end, pltpu.roll(below, end + 1, 1), last)
    for send, right in ((send_a, ceven), (send_b, jnp.logical_not(ceven))):
        back = jnp.where(right, SEG0, 0)
        for s in range(2):
            k = jnp.where(right, posf[s], negf[s])
            dy = pick(off[0], k)
            for t in range(TILES):
                total = jnp.zeros((CP, CC), f32)
                for q in range(WIN // TILES):
                    piece = window_row(dy, cb, k, t + TILES * q, has_above, has_below)
                    piece = pltpu.roll(piece.astype(f32), (SEG * q - back + CC) % CC, 1)
                    total = piece if q == 0 else jnp.where(lane >= SEG * q, piece, total)
                send[s * TILES + t] = total.astype(bf16)
        pack = jnp.where(right, last, first)
        total = pack[:CP]
        for g in range(1, C // CP):
            moved = pltpu.roll(pack[CP * g : CP * (g + 1)], TILES * g, 1)
            total = jnp.where(inner >= TILES * g, moved, total)
        send[2 * TILES] = total.astype(bf16)


def local_kernel(nrows, ncols, off, red, recv_a, recv_b, cur_t, wall, bias, part, cb, x2):
    off = scalars(off)
    above, below, has_above, has_below = row_halo(nrows, off, red, recv_a, recv_b, cb)
    col = lax.axis_index("cols")
    has_left = col > 0
    has_right = col < ncols - 1
    pos, _, _, _ = slots(off, 1)
    lane = lanes((CP, CC))
    wide = lanes((C, CC))

    def put(r, at, size, value):
        if r <= WIN - CR // 2 - 1:
            x2[r * KROW + at : r * KROW + at + size, :CC] = value
        if r >= CR // 2:
            q = r - CR // 2
            x2[q * KROW + at : q * KROW + at + size, CC:] = value

    taps = []
    for k in range(FRAMES):
        for j in range(3):
            s = off[1][k] + 1 - j
            lo = jnp.where(pos[k], s, 0)
            hi = jnp.where(pos[k], CC, CC + s)
            if j == 0:
                lo = jnp.where(has_left, lo, jnp.maximum(lo, 1))
            if j == 2:
                hi = jnp.where(has_right, hi, jnp.minimum(hi, CC - 1))
            taps.append(((s + CC) % CC, (lane >= lo) & (lane < hi)))
    for r in range(WIN):
        here = above if r == 0 else below if r == WIN - 1 else cur_t[r - 1]
        put(r, C, C, here)
        here = here.astype(f32)
        zero = jnp.zeros_like(here)
        put(r, 0, C, jnp.where(wide == 0, zero, pltpu.roll(here, 1, 1)).astype(bf16))
        put(r, 2 * C, C, jnp.where(wide == CC - 1, zero, pltpu.roll(here, CC - 1, 1)).astype(bf16))
        for k in range(FRAMES):
            own = window_row(off[0][k], cb, k, r, has_above, has_below).astype(f32)
            for j in range(3):
                s, mask = taps[3 * k + j]
                v = jnp.where(mask, pltpu.roll(own, s, 1), jnp.zeros_like(own))
                put(r, 3 * C + j * FRAMES * CP + k * CP, CP, v.astype(bf16))
    x2[(WIN - CR // 2) * KROW :, :] = jnp.zeros((KALL - 3 * KROW, 2 * CC), bf16)
    bias_col = jnp.broadcast_to(bias[...], (C, 2 * CC))
    for y in range(CR // 2):
        p = jnp.dot(
            wall[...], x2[y * KROW : y * KROW + KALL, :], preferred_element_type=f32
        )
        part[y] = p + bias_col


def finish_kernel(ncols, off, recv_a, recv_b, part, wedge, out, xx, acc):
    off = scalars(off)
    col = lax.axis_index("cols")
    ceven = col % 2 == 0
    has_left = col > 0
    has_right = col < ncols - 1
    pos, _, _, place = slots(off, 1)
    inner = segment_lane((CP, CC))
    zero = jnp.zeros((CP, CC), bf16)
    cur_a = recv_a[2 * TILES].astype(f32)
    cur_b = recv_b[2 * TILES].astype(f32)
    left = jnp.where(ceven, cur_b, cur_a)
    right = jnp.where(ceven, cur_a, cur_b)
    left = jnp.where(has_left, left, jnp.zeros_like(left))
    right = jnp.where(has_right, right, jnp.zeros_like(right))
    frames = []
    for k in range(FRAMES):
        use_a = jnp.logical_xor(pos[k], ceven)
        ok = jnp.where(pos[k], has_left, has_right)
        tiles = []
        for t in range(TILES):
            v = jnp.where(use_a, recv_a[place[k] * TILES + t], recv_b[place[k] * TILES + t])
            tiles.append(jnp.where(ok, v, zero).astype(f32))
        masks = []
        for j in range(3):
            s = off[1][k] + 1 - j
            lo = jnp.where(pos[k], 0, SEG + s)
            hi = jnp.where(pos[k], s, SEG)
            mask = (inner >= lo) & (inner < hi)
            masks.append((jnp.where(pos[k], s - SEG, s + SEG), mask))
        frames.append((tiles, masks))
    for u in range(TILES + 2):
        base = u * EROW
        back = SEG * (u // TILES)
        shift = back + u % TILES
        for g in range(C // CP):
            rows = slice(base + g * CP, base + (g + 1) * CP)
            v = pltpu.roll(left, (2 * CC - shift - TILES * g) % CC, 1)
            xx[rows, :CC] = jnp.where(inner == 0, v, 0.0).astype(bf16)
            xx[rows, CC:] = zero
            rows = slice(base + C + g * CP, base + C + (g + 1) * CP)
            v = pltpu.roll(right, (2 * CC + SEG - 1 - shift - TILES * g) % CC, 1)
            xx[rows, :CC] = zero
            xx[rows, CC:] = jnp.where(inner == SEG - 1, v, 0.0).astype(bf16)
        for k in range(FRAMES):
            tiles, masks = frames[k]
            for j in range(3):
                move, mask = masks[j]
                v = pltpu.roll(tiles[u % TILES], (move - back + 2 * CC) % CC, 1)
                v = jnp.where(mask, v, 0.0).astype(bf16)
                at = base + 2 * C + j * FRAMES * CP + k * CP
                xx[at : at + CP, :CC] = jnp.where(pos[k], v, zero)
                xx[at : at + CP, CC:] = jnp.where(pos[k], zero, v)
    xx[(TILES + 2) * EROW :, :] = jnp.zeros((KEDGE - 3 * EROW, 2 * CC), bf16)
    wide = lanes((C, CC))
    for t in range(TILES):
        p = jnp.dot(
            wedge[...], xx[t * EROW : t * EROW + KEDGE, :], preferred_element_type=f32
        )
        for y in range(t, CR, TILES):
            q = y // TILES
            lft = pltpu.roll(p[:, :CC], (CC - SEG * q) % CC, 1)
            rgt = pltpu.roll(p[:, CC:], (SEG0 - SEG * q) % CC, 1)
            v = jnp.where(wide < SEG, lft, jnp.where(wide >= SEG0, rgt, 0.0))
            at = 0 if y < CR // 2 else CC
            v = jnp.maximum(part[y % (CR // 2), :, at : at + CC] + v, 0.0)
            acc[pl.ds(y, C, stride=CR), :] = v
    out[...] = acc[...].astype(bf16)


def swap(x, axis, shifted):
    size = lax.axis_size(axis)
    if shifted:
        pairs = [(i, (i - 1 if i % 2 == 0 else i + 1) % size) for i in range(size)]
    else:
        pairs = [(i, i ^ 1) for i in range(size)]
    return lax.ppermute(x, axis, pairs)


def cost(flops, bytes_accessed):
    return pl.CostEstimate(flops=flops, bytes_accessed=bytes_accessed, transcendentals=0)


def call(kernel, outs, specs, scratch, estimate):
    vmem = pl.BlockSpec(memory_space=pltpu.VMEM)
    return pl.pallas_call(
        kernel,
        out_shape=[jax.ShapeDtypeStruct(*out) for out in outs],
        in_specs=specs,
        out_specs=[vmem] * len(outs),
        scratch_shapes=scratch,
        cost_estimate=estimate,
        compiler_params=pltpu.CompilerParams(vmem_limit_bytes=VMEM_LIMIT),
    )


def body(current_frame, history_frames, offsets, compress_weight, mixer_weight, mixer_bias):
    vmem = pl.BlockSpec(memory_space=pltpu.VMEM)
    hbm = pl.BlockSpec(memory_space=pltpu.HBM)
    off = offsets.T
    hist = history_frames.reshape(FRAMES, C * CR, CC)
    cur = current_frame.reshape(C * CR, CC)
    wt = mixer_weight.transpose(0, 1, 3, 2)
    nrows, ncols = lax.axis_size("rows"), lax.axis_size("cols")
    row_send = (2 * REACH + C // CP, CP, CC)
    col_send = (2 * TILES + 1, CP, CC)
    red, send_a, send_b = call(
        compress_kernel,
        [((FRAMES, CR, CP, CC), bf16), (row_send, bf16), (row_send, bf16)],
        [hbm] * 4,
        [
            pltpu.SMEM((2, FRAMES), jnp.int32),
            pltpu.VMEM((CP, C), bf16),
            pltpu.VMEM((FRAMES, C * CR, CC), bf16),
            pltpu.VMEM((C * CR, CC), bf16),
            pltpu.VMEM((FRAMES, C * CR, CC), f32),
            pltpu.SemaphoreType.DMA((FRAMES + 3,)),
        ],
        cost(2 * FRAMES * CP * C * CR * CC, 3 << 20),
    )(*[pltpu.with_memory_space_constraint(v, pltpu.HBM) for v in (off, hist, cur, compress_weight)])
    recv_a = swap(send_a, "rows", False)
    recv_b = swap(send_b, "rows", True)
    cur_t, cols, wall, wedge = call(
        prepare_kernel,
        [((CR, C, CC), bf16), ((2, C, CC), bf16), ((C, KALL), bf16), ((C, KEDGE), bf16)],
        [vmem, vmem],
        [pltpu.VMEM((C * CR, CC), f32)],
        cost(1 << 20, 3 << 20),
    )(cur, wt)
    halo_rows = pltpu.VMEM((FRAMES, CR + 2 * REACH, CP, CC), bf16)
    csend_a, csend_b = call(
        lambda *refs: pack_kernel(nrows, *refs),
        [(col_send, bf16), (col_send, bf16)],
        [vmem] * 5,
        [halo_rows],
        cost(1 << 20, 2 << 20),
    )(off, red, recv_a, recv_b, cols)
    crecv_a = swap(csend_a, "cols", False)
    crecv_b = swap(csend_b, "cols", True)
    (part,) = call(
        lambda *refs: local_kernel(nrows, ncols, *refs),
        [((CR // 2, C, 2 * CC), f32)],
        [vmem] * 7,
        [halo_rows, pltpu.VMEM(((WIN - CR // 2) * KROW + KALL - 3 * KROW, 2 * CC), bf16)],
        cost(2 * C * KALL * CR * CC, 4 << 20),
    )(off, red, recv_a, recv_b, cur_t, wall, mixer_bias.reshape(C, 1))
    (out,) = call(
        lambda *refs: finish_kernel(ncols, *refs),
        [((C * CR, CC), bf16)],
        [vmem] * 5,
        [
            pltpu.VMEM(((TILES + 2) * EROW + KEDGE - 3 * EROW, 2 * CC), bf16),
            pltpu.VMEM((C * CR, CC), f32),
        ],
        cost(1 << 20, 2 << 20),
    )(off, crecv_a, crecv_b, part, wedge)
    return out.reshape(C, CR, CC)


def solution(mesh):
    in_specs = (P(None, "rows", "cols"), P(None, None, "rows", "cols"), P(), P(), P(), P())
    out_specs = P(None, "rows", "cols")
    return jax.shard_map(body, mesh=mesh, in_specs=in_specs, out_specs=out_specs, check_vma=False)
```

```python
import jax
import jax.numpy as jnp
from jax import lax
from jax.experimental import pallas as pl
from jax.experimental.pallas import tpu as pltpu
from jax.sharding import PartitionSpec as P

C = 128
CP = 32
FRAMES = 3
CR = 16
CC = 128
SHIFT_X = 16
SHIFT_Y = 8
REACH = SHIFT_Y + 1
WIN = CR + 2
KROW = 3 * C + 3 * FRAMES * CP
KALL = 2048
EROW = 2 * C + 3 * FRAMES * CP
KEDGE = 1664
TILES = 3
SEG = 21
SEG0 = CC - SEG
VMEM_LIMIT = 48 * 1024 * 1024
f32 = jnp.float32
bf16 = jnp.bfloat16


def slots(off, axis):
    pos = [off[axis][k] > 0 for k in range(FRAMES)]
    first_pos = jnp.where(pos[0], 0, jnp.where(pos[1], 1, 2))
    last_pos = jnp.where(pos[2], 2, jnp.where(pos[1], 1, 0))
    first_neg = jnp.where(pos[0], jnp.where(pos[1], 2, 1), 0)
    last_neg = jnp.where(pos[2], jnp.where(pos[1], 0, 1), 2)
    place = [
        jnp.where(pos[k], jnp.where(first_pos == k, 0, 1), jnp.where(first_neg == k, 0, 1))
        for k in range(FRAMES)
    ]
    return pos, (first_pos, last_pos), (first_neg, last_neg), place


def scalars(ref):
    return [[ref[axis, k] for k in range(FRAMES)] for axis in range(2)]


def pick(values, k):
    return jnp.where(k == 0, values[0], jnp.where(k == 1, values[1], values[2]))


def lanes(shape):
    return lax.broadcasted_iota(jnp.int32, shape, len(shape) - 1)


def compress_kernel(
    off_hbm, hist, cur, w_hbm, red, send_a, send_b, off, w, hbuf, cbuf, sems
):
    copies = [pltpu.make_async_copy(hist.at[k], hbuf.at[k], sems.at[k]) for k in range(FRAMES)]
    copies.append(pltpu.make_async_copy(cur, cbuf, sems.at[FRAMES]))
    small = [
        pltpu.make_async_copy(w_hbm, w, sems.at[FRAMES + 1]),
        pltpu.make_async_copy(off_hbm, off, sems.at[FRAMES + 2]),
    ]
    for copy in small[:1] + copies + small[1:]:
        copy.start()
    row = lax.axis_index("rows")
    even = row % 2 == 0
    small[0].wait()
    for k in range(FRAMES):
        copies[k].wait()
        by_row = jnp.swapaxes(hbuf[k].reshape(C, CR, CC), 0, 1)
        x = jnp.concatenate([by_row[y] for y in range(CR)], axis=1)
        r = jnp.dot(w[...], x, preferred_element_type=f32).astype(bf16)
        for y in range(CR):
            red[k, y] = r[:, y * CC : (y + 1) * CC]
    copies[FRAMES].wait()
    by_row = jnp.swapaxes(cbuf[...].reshape(C, CR, CC), 0, 1)
    top = by_row[0].reshape(C // CP, CP, CC)
    bottom = by_row[CR - 1].reshape(C // CP, CP, CC)
    small[1].wait()
    _, posf, negf, _ = slots(scalars(off), 0)
    for send, down in ((send_a, even), (send_b, jnp.logical_not(even))):
        start = jnp.where(down, CR - REACH, 0)
        for s in range(2):
            k = jnp.where(down, posf[s], negf[s])
            for i in range(REACH):
                send[s * REACH + i] = red[k, start + i]
        send[2 * REACH : 2 * REACH + C // CP] = jnp.where(down, bottom, top)


def spot(r):
    return SEG * (r // TILES) + r % TILES


def segment_lane(shape):
    lane = lanes(shape)
    base = jnp.zeros(shape, jnp.int32)
    for m in range(1, CC // SEG + 1):
        base = jnp.where(lane >= SEG * m, SEG * m, base)
    return lane - base


def prepare_kernel(cur, wt, cur_t, cols, wall, wedge, fbuf):
    fbuf[...] = cur[...].astype(f32)
    lane = lanes((C, CC))
    first = jnp.zeros((C, CC), f32)
    last = jnp.zeros((C, CC), f32)
    for y in range(CR):
        t = fbuf[pl.ds(y, C, stride=CR), :]
        cur_t[y] = t.astype(bf16)
        at = spot(y + 1)
        first = jnp.where(lane == at, pltpu.roll(t, at, 1), first)
        last = jnp.where(lane == at, pltpu.roll(t, at + 1, 1), last)
    cols[0] = first.astype(bf16)
    cols[1] = last.astype(bf16)
    for dest, taps, size in ((wall, (0, 1, 2), KALL), (wedge, (0, 2), KEDGE)):
        parts = []
        for i in range(3):
            parts += [wt[i, j, :C, :] for j in taps]
            parts += [wt[i, j, C:, :] for j in range(3)]
        parts.append(jnp.zeros((size - sum(p.shape[0] for p in parts), C), bf16))
        tall = jnp.concatenate(parts, axis=0).astype(f32)
        for b in range(size // C):
            dest[:, b * C : (b + 1) * C] = tall[b * C : (b + 1) * C].T.astype(bf16)


def row_halo(nrows, off, red, recv_a, recv_b, cb):
    row = lax.axis_index("rows")
    even = row % 2 == 0
    has_above = row > 0
    has_below = row < nrows - 1
    pos, _, _, place = slots(off, 0)
    zero = jnp.zeros((REACH, CP, CC), bf16)
    for k in range(FRAMES):
        cb[k, REACH : REACH + CR] = red[k]
        at = pl.ds(place[k] * REACH, REACH)
        from_a = recv_a[at]
        from_b = recv_b[at]
        use_a = jnp.logical_xor(pos[k], even)
        ok = jnp.where(pos[k], has_above, has_below)
        halo = jnp.where(ok, jnp.where(use_a, from_a, from_b), zero)
        cb[k, pl.ds(jnp.where(pos[k], 0, REACH + CR), REACH)] = halo
    tail_a = recv_a[2 * REACH : 2 * REACH + C // CP].reshape(C, CC)
    tail_b = recv_b[2 * REACH : 2 * REACH + C // CP].reshape(C, CC)
    blank = jnp.zeros((C, CC), bf16)
    above = jnp.where(has_above, jnp.where(even, tail_b, tail_a), blank)
    below = jnp.where(has_below, jnp.where(even, tail_a, tail_b), blank)
    return above, below, has_above, has_below


def window_row(dy, cb, k, r, has_above, has_below):
    v = cb[k, SHIFT_Y - dy + r]
    if r == 0:
        v = jnp.where(has_above, v, jnp.zeros_like(v))
    if r == WIN - 1:
        v = jnp.where(has_below, v, jnp.zeros_like(v))
    return v


def pack_kernel(nrows, off, red, recv_a, recv_b, cols, send_a, send_b, cb):
    off = scalars(off)
    above, below, has_above, has_below = row_halo(nrows, off, red, recv_a, recv_b, cb)
    above = above.astype(f32)
    below = below.astype(f32)
    ceven = lax.axis_index("cols") % 2 == 0
    _, posf, negf, _ = slots(off, 1)
    lane = lanes((CP, CC))
    inner = segment_lane((CP, CC))
    wide = lanes((C, CC))
    end = spot(WIN - 1)
    first = jnp.where(wide == 0, above, cols[0].astype(f32))
    first = jnp.where(wide == end, pltpu.roll(below, end, 1), first)
    last = jnp.where(wide == 0, pltpu.roll(above, 1, 1), cols[1].astype(f32))
    last = jnp.where(wide == end, pltpu.roll(below, end + 1, 1), last)
    for send, right in ((send_a, ceven), (send_b, jnp.logical_not(ceven))):
        back = jnp.where(right, SEG0, 0)
        for s in range(2):
            k = jnp.where(right, posf[s], negf[s])
            dy = pick(off[0], k)
            for t in range(TILES):
                total = jnp.zeros((CP, CC), f32)
                for q in range(WIN // TILES):
                    piece = window_row(dy, cb, k, t + TILES * q, has_above, has_below)
                    piece = pltpu.roll(piece.astype(f32), (SEG * q - back + CC) % CC, 1)
                    total = piece if q == 0 else jnp.where(lane >= SEG * q, piece, total)
                send[s * TILES + t] = total.astype(bf16)
        pack = jnp.where(right, last, first)
        total = pack[:CP]
        for g in range(1, C // CP):
            moved = pltpu.roll(pack[CP * g : CP * (g + 1)], TILES * g, 1)
            total = jnp.where(inner >= TILES * g, moved, total)
        send[2 * TILES] = total.astype(bf16)


def local_kernel(nrows, ncols, off, red, recv_a, recv_b, cur_t, wall, bias, part, cb, x2):
    off = scalars(off)
    above, below, has_above, has_below = row_halo(nrows, off, red, recv_a, recv_b, cb)
    col = lax.axis_index("cols")
    has_left = col > 0
    has_right = col < ncols - 1
    pos, _, _, _ = slots(off, 1)
    lane = lanes((CP, CC))
    wide = lanes((C, CC))

    def put(r, at, size, value):
        if r <= WIN - CR // 2 - 1:
            x2[r * KROW + at : r * KROW + at + size, :CC] = value
        if r >= CR // 2:
            q = r - CR // 2
            x2[q * KROW + at : q * KROW + at + size, CC:] = value

    taps = []
    for k in range(FRAMES):
        for j in range(3):
            s = off[1][k] + 1 - j
            lo = jnp.where(pos[k], s, 0)
            hi = jnp.where(pos[k], CC, CC + s)
            if j == 0:
                lo = jnp.where(has_left, lo, jnp.maximum(lo, 1))
            if j == 2:
                hi = jnp.where(has_right, hi, jnp.minimum(hi, CC - 1))
            taps.append(((s + CC) % CC, (lane >= lo) & (lane < hi)))
    for r in range(WIN):
        here = above if r == 0 else below if r == WIN - 1 else cur_t[r - 1]
        put(r, C, C, here)
        here = here.astype(f32)
        zero = jnp.zeros_like(here)
        put(r, 0, C, jnp.where(wide == 0, zero, pltpu.roll(here, 1, 1)).astype(bf16))
        put(r, 2 * C, C, jnp.where(wide == CC - 1, zero, pltpu.roll(here, CC - 1, 1)).astype(bf16))
        for k in range(FRAMES):
            own = window_row(off[0][k], cb, k, r, has_above, has_below).astype(f32)
            for j in range(3):
                s, mask = taps[3 * k + j]
                v = jnp.where(mask, pltpu.roll(own, s, 1), jnp.zeros_like(own))
                put(r, 3 * C + j * FRAMES * CP + k * CP, CP, v.astype(bf16))
    x2[(WIN - CR // 2) * KROW :, :] = jnp.zeros((KALL - 3 * KROW, 2 * CC), bf16)
    bias_col = jnp.broadcast_to(bias[...], (C, 2 * CC))
    for y in range(CR // 2):
        p = jnp.dot(
            wall[...], x2[y * KROW : y * KROW + KALL, :], preferred_element_type=f32
        )
        part[y] = p + bias_col


def finish_kernel(ncols, off, recv_b, recv_a, part, wedge, out, xx, acc):
    off = scalars(off)
    col = lax.axis_index("cols")
    ceven = col % 2 == 0
    has_left = col > 0
    has_right = col < ncols - 1
    pos, _, _, place = slots(off, 1)
    inner = segment_lane((CP, CC))
    zero = jnp.zeros((CP, CC), bf16)
    cur_a = recv_a[2 * TILES].astype(f32)
    cur_b = recv_b[2 * TILES].astype(f32)
    left = jnp.where(ceven, cur_b, cur_a)
    right = jnp.where(ceven, cur_a, cur_b)
    left = jnp.where(has_left, left, jnp.zeros_like(left))
    right = jnp.where(has_right, right, jnp.zeros_like(right))
    frames = []
    for k in range(FRAMES):
        use_a = jnp.logical_xor(pos[k], ceven)
        ok = jnp.where(pos[k], has_left, has_right)
        tiles = []
        for t in range(TILES):
            v = jnp.where(use_a, recv_a[place[k] * TILES + t], recv_b[place[k] * TILES + t])
            tiles.append(jnp.where(ok, v, zero).astype(f32))
        masks = []
        for j in range(3):
            s = off[1][k] + 1 - j
            lo = jnp.where(pos[k], 0, SEG + s)
            hi = jnp.where(pos[k], s, SEG)
            mask = (inner >= lo) & (inner < hi)
            masks.append((jnp.where(pos[k], s - SEG, s + SEG), mask))
        frames.append((tiles, masks))
    for u in range(TILES + 2):
        base = u * EROW
        back = SEG * (u // TILES)
        shift = back + u % TILES
        for g in range(C // CP):
            rows = slice(base + g * CP, base + (g + 1) * CP)
            v = pltpu.roll(left, (2 * CC - shift - TILES * g) % CC, 1)
            xx[rows, :CC] = jnp.where(inner == 0, v, 0.0).astype(bf16)
            xx[rows, CC:] = zero
            rows = slice(base + C + g * CP, base + C + (g + 1) * CP)
            v = pltpu.roll(right, (2 * CC + SEG - 1 - shift - TILES * g) % CC, 1)
            xx[rows, :CC] = zero
            xx[rows, CC:] = jnp.where(inner == SEG - 1, v, 0.0).astype(bf16)
        for k in range(FRAMES):
            tiles, masks = frames[k]
            for j in range(3):
                move, mask = masks[j]
                v = pltpu.roll(tiles[u % TILES], (move - back + 2 * CC) % CC, 1)
                v = jnp.where(mask, v, 0.0).astype(bf16)
                at = base + 2 * C + j * FRAMES * CP + k * CP
                xx[at : at + CP, :CC] = jnp.where(pos[k], v, zero)
                xx[at : at + CP, CC:] = jnp.where(pos[k], zero, v)
    xx[(TILES + 2) * EROW :, :] = jnp.zeros((KEDGE - 3 * EROW, 2 * CC), bf16)
    wide = lanes((C, CC))
    for t in range(TILES):
        p = jnp.dot(
            wedge[...], xx[t * EROW : t * EROW + KEDGE, :], preferred_element_type=f32
        )
        for y in range(t, CR, TILES):
            q = y // TILES
            lft = pltpu.roll(p[:, :CC], (CC - SEG * q) % CC, 1)
            rgt = pltpu.roll(p[:, CC:], (SEG0 - SEG * q) % CC, 1)
            v = jnp.where(wide < SEG, lft, jnp.where(wide >= SEG0, rgt, 0.0))
            at = 0 if y < CR // 2 else CC
            v = jnp.maximum(part[y % (CR // 2), :, at : at + CC] + v, 0.0)
            acc[pl.ds(y, C, stride=CR), :] = v
    out[...] = acc[...].astype(bf16)


def partner(i, size, shifted):
    if not shifted:
        return i ^ 1
    j = i - 1 if i % 2 == 0 else i + 1
    return j if 0 <= j < size else None


def swap(x, axis, shifted):
    nrows, ncols = lax.axis_size("rows"), lax.axis_size("cols")
    pairs = []
    for r in range(nrows):
        for c in range(ncols):
            if axis == "rows":
                to = partner(r, nrows, shifted)
                to = (r, c ^ 1) if to is None else (to, c)
            else:
                to = partner(c, ncols, shifted)
                to = (r ^ 1, c) if to is None else (r, to)
            pairs.append((r * ncols + c, to[0] * ncols + to[1]))
    return lax.ppermute(x, ("rows", "cols"), pairs)


def cost(flops, bytes_accessed):
    return pl.CostEstimate(flops=flops, bytes_accessed=bytes_accessed, transcendentals=0)


def call(kernel, outs, specs, scratch, estimate):
    vmem = pl.BlockSpec(memory_space=pltpu.VMEM)
    return pl.pallas_call(
        kernel,
        out_shape=[jax.ShapeDtypeStruct(*out) for out in outs],
        in_specs=specs,
        out_specs=[vmem] * len(outs),
        scratch_shapes=scratch,
        cost_estimate=estimate,
        compiler_params=pltpu.CompilerParams(vmem_limit_bytes=VMEM_LIMIT),
    )


def body(current_frame, history_frames, offsets, compress_weight, mixer_weight, mixer_bias):
    vmem = pl.BlockSpec(memory_space=pltpu.VMEM)
    hbm = pl.BlockSpec(memory_space=pltpu.HBM)
    off = offsets.T
    hist = history_frames.reshape(FRAMES, C * CR, CC)
    cur = current_frame.reshape(C * CR, CC)
    wt = mixer_weight.transpose(0, 1, 3, 2)
    nrows, ncols = lax.axis_size("rows"), lax.axis_size("cols")
    row_send = (2 * REACH + C // CP, CP, CC)
    col_send = (2 * TILES + 1, CP, CC)
    red, send_a, send_b = call(
        compress_kernel,
        [((FRAMES, CR, CP, CC), bf16), (row_send, bf16), (row_send, bf16)],
        [hbm] * 4,
        [
            pltpu.SMEM((2, FRAMES), jnp.int32),
            pltpu.VMEM((CP, C), bf16),
            pltpu.VMEM((FRAMES, C * CR, CC), bf16),
            pltpu.VMEM((C * CR, CC), bf16),
            pltpu.SemaphoreType.DMA((FRAMES + 3,)),
        ],
        cost(2 * FRAMES * CP * C * CR * CC, 3 << 20),
    )(*[pltpu.with_memory_space_constraint(v, pltpu.HBM) for v in (off, hist, cur, compress_weight)])
    recv_a = swap(send_a, "rows", False)
    recv_b = swap(send_b, "rows", True)
    cur_t, cols, wall, wedge = call(
        prepare_kernel,
        [((CR, C, CC), bf16), ((2, C, CC), bf16), ((C, KALL), bf16), ((C, KEDGE), bf16)],
        [vmem, vmem],
        [pltpu.VMEM((C * CR, CC), f32)],
        cost(1 << 20, 3 << 20),
    )(cur, wt)
    halo_rows = pltpu.VMEM((FRAMES, CR + 2 * REACH, CP, CC), bf16)
    csend_a, csend_b = call(
        lambda *refs: pack_kernel(nrows, *refs),
        [(col_send, bf16), (col_send, bf16)],
        [vmem] * 5,
        [halo_rows],
        cost(1 << 20, 2 << 20),
    )(off, red, recv_a, recv_b, cols)
    crecv_b = swap(csend_b, "cols", True)
    crecv_a = swap(csend_a, "cols", False)
    (part,) = call(
        lambda *refs: local_kernel(nrows, ncols, *refs),
        [((CR // 2, C, 2 * CC), f32)],
        [vmem] * 7,
        [halo_rows, pltpu.VMEM(((WIN - CR // 2) * KROW + KALL - 3 * KROW, 2 * CC), bf16)],
        cost(2 * C * KALL * CR * CC, 4 << 20),
    )(off, red, recv_a, recv_b, cur_t, wall, mixer_bias.reshape(C, 1))
    (out,) = call(
        lambda *refs: finish_kernel(ncols, *refs),
        [((C * CR, CC), bf16)],
        [vmem] * 5,
        [
            pltpu.VMEM(((TILES + 2) * EROW + KEDGE - 3 * EROW, 2 * CC), bf16),
            pltpu.VMEM((C * CR, CC), f32),
        ],
        cost(1 << 20, 2 << 20),
    )(off, crecv_b, crecv_a, part, wedge)
    return out.reshape(C, CR, CC)


def solution(mesh):
    in_specs = (P(None, "rows", "cols"), P(None, None, "rows", "cols"), P(), P(), P(), P())
    out_specs = P(None, "rows", "cols")
    return jax.shard_map(body, mesh=mesh, in_specs=in_specs, out_specs=out_specs, check_vma=False)
```

```python
import jax
import jax.numpy as jnp
from jax import lax
from jax.experimental import pallas as pl
from jax.experimental.pallas import tpu as pltpu
from jax.sharding import PartitionSpec as P

C = 128
CP = 32
FRAMES = 3
CR = 16
CC = 128
SHIFT_X = 16
SHIFT_Y = 8
REACH = SHIFT_Y + 1
WIN = CR + 2
KROW = 3 * C + 3 * FRAMES * CP
KALL = 2048
PARTS = 4
EROW = 2 * C + 3 * FRAMES * CP
KEDGE = 1664
TILES = 3
SEG = 21
SEG0 = CC - SEG
VMEM_LIMIT = 48 * 1024 * 1024
f32 = jnp.float32
bf16 = jnp.bfloat16


def slots(off, axis):
    pos = [off[axis][k] > 0 for k in range(FRAMES)]
    first_pos = jnp.where(pos[0], 0, jnp.where(pos[1], 1, 2))
    last_pos = jnp.where(pos[2], 2, jnp.where(pos[1], 1, 0))
    first_neg = jnp.where(pos[0], jnp.where(pos[1], 2, 1), 0)
    last_neg = jnp.where(pos[2], jnp.where(pos[1], 0, 1), 2)
    place = [
        jnp.where(pos[k], jnp.where(first_pos == k, 0, 1), jnp.where(first_neg == k, 0, 1))
        for k in range(FRAMES)
    ]
    return pos, (first_pos, last_pos), (first_neg, last_neg), place


def scalars(ref):
    return [[ref[axis, k] for k in range(FRAMES)] for axis in range(2)]


def pick(values, k):
    return jnp.where(k == 0, values[0], jnp.where(k == 1, values[1], values[2]))


def lanes(shape):
    return lax.broadcasted_iota(jnp.int32, shape, len(shape) - 1)


def compress_kernel(
    off_hbm, hist, cur, w_hbm, red, send_a, send_b, off, w, hbuf, cbuf, sems
):
    copies = [pltpu.make_async_copy(hist.at[k], hbuf.at[k], sems.at[k]) for k in range(FRAMES)]
    copies.append(pltpu.make_async_copy(cur, cbuf, sems.at[FRAMES]))
    small = [
        pltpu.make_async_copy(w_hbm, w, sems.at[FRAMES + 1]),
        pltpu.make_async_copy(off_hbm, off, sems.at[FRAMES + 2]),
    ]
    for copy in small[:1] + copies + small[1:]:
        copy.start()
    row = lax.axis_index("rows")
    even = row % 2 == 0
    small[0].wait()
    for k in range(FRAMES):
        copies[k].wait()
        by_row = jnp.swapaxes(hbuf[k].reshape(C, CR, CC), 0, 1)
        x = jnp.concatenate([by_row[y] for y in range(CR)], axis=1)
        r = jnp.dot(w[...], x, preferred_element_type=f32).astype(bf16)
        for y in range(CR):
            red[k, y] = r[:, y * CC : (y + 1) * CC]
    copies[FRAMES].wait()
    by_row = jnp.swapaxes(cbuf[...].reshape(C, CR, CC), 0, 1)
    top = by_row[0].reshape(C // CP, CP, CC)
    bottom = by_row[CR - 1].reshape(C // CP, CP, CC)
    small[1].wait()
    _, posf, negf, _ = slots(scalars(off), 0)
    for send, down in ((send_a, even), (send_b, jnp.logical_not(even))):
        start = jnp.where(down, CR - REACH, 0)
        for s in range(2):
            k = jnp.where(down, posf[s], negf[s])
            for i in range(REACH):
                send[s * REACH + i] = red[k, start + i]
        send[2 * REACH : 2 * REACH + C // CP] = jnp.where(down, bottom, top)


def spot(r):
    return SEG * (r // TILES) + r % TILES


def segment_lane(shape):
    lane = lanes(shape)
    base = jnp.zeros(shape, jnp.int32)
    for m in range(1, CC // SEG + 1):
        base = jnp.where(lane >= SEG * m, SEG * m, base)
    return lane - base


def prepare_kernel(cur, wt, cur_t, cols, wall, wedge, fbuf):
    fbuf[...] = cur[...].astype(f32)
    lane = lanes((C, CC))
    first = jnp.zeros((C, CC), f32)
    last = jnp.zeros((C, CC), f32)
    for y in range(CR):
        t = fbuf[pl.ds(y, C, stride=CR), :]
        cur_t[y] = t.astype(bf16)
        at = spot(y + 1)
        first = jnp.where(lane == at, pltpu.roll(t, at, 1), first)
        last = jnp.where(lane == at, pltpu.roll(t, at + 1, 1), last)
    cols[0] = first.astype(bf16)
    cols[1] = last.astype(bf16)
    for dest, taps, size in ((wall, (0, 1, 2), KALL), (wedge, (0, 2), KEDGE)):
        parts = []
        for i in range(3):
            parts += [wt[i, j, :C, :] for j in taps]
            parts += [wt[i, j, C:, :] for j in range(3)]
        parts.append(jnp.zeros((size - sum(p.shape[0] for p in parts), C), bf16))
        tall = jnp.concatenate(parts, axis=0).astype(f32)
        for b in range(size // C):
            dest[:, b * C : (b + 1) * C] = tall[b * C : (b + 1) * C].T.astype(bf16)


def row_halo(nrows, off, red, recv_a, recv_b, cb):
    row = lax.axis_index("rows")
    even = row % 2 == 0
    has_above = row > 0
    has_below = row < nrows - 1
    pos, _, _, place = slots(off, 0)
    zero = jnp.zeros((REACH, CP, CC), bf16)
    for k in range(FRAMES):
        cb[k, REACH : REACH + CR] = red[k]
        at = pl.ds(place[k] * REACH, REACH)
        from_a = recv_a[at]
        from_b = recv_b[at]
        use_a = jnp.logical_xor(pos[k], even)
        ok = jnp.where(pos[k], has_above, has_below)
        halo = jnp.where(ok, jnp.where(use_a, from_a, from_b), zero)
        cb[k, pl.ds(jnp.where(pos[k], 0, REACH + CR), REACH)] = halo
    tail_a = recv_a[2 * REACH : 2 * REACH + C // CP].reshape(C, CC)
    tail_b = recv_b[2 * REACH : 2 * REACH + C // CP].reshape(C, CC)
    blank = jnp.zeros((C, CC), bf16)
    above = jnp.where(has_above, jnp.where(even, tail_b, tail_a), blank)
    below = jnp.where(has_below, jnp.where(even, tail_a, tail_b), blank)
    return above, below, has_above, has_below


def window_row(dy, cb, k, r, has_above, has_below):
    v = cb[k, SHIFT_Y - dy + r]
    if r == 0:
        v = jnp.where(has_above, v, jnp.zeros_like(v))
    if r == WIN - 1:
        v = jnp.where(has_below, v, jnp.zeros_like(v))
    return v


def pack_kernel(nrows, off, red, recv_b, recv_a, cols, send_a, send_b, cb):
    off = scalars(off)
    above, below, has_above, has_below = row_halo(nrows, off, red, recv_a, recv_b, cb)
    above = above.astype(f32)
    below = below.astype(f32)
    ceven = lax.axis_index("cols") % 2 == 0
    _, posf, negf, _ = slots(off, 1)
    lane = lanes((CP, CC))
    inner = segment_lane((CP, CC))
    wide = lanes((C, CC))
    end = spot(WIN - 1)
    first = jnp.where(wide == 0, above, cols[0].astype(f32))
    first = jnp.where(wide == end, pltpu.roll(below, end, 1), first)
    last = jnp.where(wide == 0, pltpu.roll(above, 1, 1), cols[1].astype(f32))
    last = jnp.where(wide == end, pltpu.roll(below, end + 1, 1), last)
    for send, right in ((send_a, ceven), (send_b, jnp.logical_not(ceven))):
        back = jnp.where(right, SEG0, 0)
        for s in range(2):
            k = jnp.where(right, posf[s], negf[s])
            dy = pick(off[0], k)
            for t in range(TILES):
                total = jnp.zeros((CP, CC), f32)
                for q in range(WIN // TILES):
                    piece = window_row(dy, cb, k, t + TILES * q, has_above, has_below)
                    piece = pltpu.roll(piece.astype(f32), (SEG * q - back + CC) % CC, 1)
                    total = piece if q == 0 else jnp.where(lane >= SEG * q, piece, total)
                send[s * TILES + t] = total.astype(bf16)
        pack = jnp.where(right, last, first)
        total = pack[:CP]
        for g in range(1, C // CP):
            moved = pltpu.roll(pack[CP * g : CP * (g + 1)], TILES * g, 1)
            total = jnp.where(inner >= TILES * g, moved, total)
        send[2 * TILES] = total.astype(bf16)


def local_kernel(nrows, ncols, off, red, recv_b, recv_a, cur_t, wall, bias, part, cb, x2):
    off = scalars(off)
    above, below, has_above, has_below = row_halo(nrows, off, red, recv_a, recv_b, cb)
    col = lax.axis_index("cols")
    has_left = col > 0
    has_right = col < ncols - 1
    pos, _, _, _ = slots(off, 1)
    lane = lanes((CP, CC))
    wide = lanes((C, CC))

    def put(r, at, size, value):
        if r <= WIN - CR // 2 - 1:
            x2[r * KROW + at : r * KROW + at + size, :CC] = value
        if r >= CR // 2:
            q = r - CR // 2
            x2[q * KROW + at : q * KROW + at + size, CC:] = value

    taps = []
    for k in range(FRAMES):
        for j in range(3):
            s = off[1][k] + 1 - j
            lo = jnp.where(pos[k], s, 0)
            hi = jnp.where(pos[k], CC, CC + s)
            if j == 0:
                lo = jnp.where(has_left, lo, jnp.maximum(lo, 1))
            if j == 2:
                hi = jnp.where(has_right, hi, jnp.minimum(hi, CC - 1))
            taps.append(((s + CC) % CC, (lane >= lo) & (lane < hi)))
    for r in range(WIN):
        here = above if r == 0 else below if r == WIN - 1 else cur_t[r - 1]
        put(r, C, C, here)
        here = here.astype(f32)
        zero = jnp.zeros_like(here)
        put(r, 0, C, jnp.where(wide == 0, zero, pltpu.roll(here, 1, 1)).astype(bf16))
        put(r, 2 * C, C, jnp.where(wide == CC - 1, zero, pltpu.roll(here, CC - 1, 1)).astype(bf16))
        for k in range(FRAMES):
            own = window_row(off[0][k], cb, k, r, has_above, has_below).astype(f32)
            for j in range(3):
                s, mask = taps[3 * k + j]
                v = jnp.where(mask, pltpu.roll(own, s, 1), jnp.zeros_like(own))
                put(r, 3 * C + j * FRAMES * CP + k * CP, CP, v.astype(bf16))
    x2[(WIN - CR // 2) * KROW :, :] = jnp.zeros((KALL - 3 * KROW, 2 * CC), bf16)
    bias_col = jnp.broadcast_to(bias[...], (C, 2 * CC))
    for y in range(CR // 2):
        p = jnp.dot(
            wall[...], x2[y * KROW : y * KROW + KALL, :], preferred_element_type=f32
        )
        part[y] = p + bias_col


def finish_kernel(ncols, off, recv_b, recv_a, part, wedge, out, xx, acc, corr, done, sems):
    off = scalars(off)
    col = lax.axis_index("cols")
    ceven = col % 2 == 0
    has_left = col > 0
    has_right = col < ncols - 1
    pos, _, _, place = slots(off, 1)
    inner = segment_lane((CP, CC))
    zero = jnp.zeros((CP, CC), bf16)
    cur_a = recv_a[2 * TILES].astype(f32)
    cur_b = recv_b[2 * TILES].astype(f32)
    left = jnp.where(ceven, cur_b, cur_a)
    right = jnp.where(ceven, cur_a, cur_b)
    left = jnp.where(has_left, left, jnp.zeros_like(left))
    right = jnp.where(has_right, right, jnp.zeros_like(right))
    frames = []
    for k in range(FRAMES):
        use_a = jnp.logical_xor(pos[k], ceven)
        ok = jnp.where(pos[k], has_left, has_right)
        tiles = []
        for t in range(TILES):
            v = jnp.where(use_a, recv_a[place[k] * TILES + t], recv_b[place[k] * TILES + t])
            tiles.append(jnp.where(ok, v, zero).astype(f32))
        masks = []
        for j in range(3):
            s = off[1][k] + 1 - j
            lo = jnp.where(pos[k], 0, SEG + s)
            hi = jnp.where(pos[k], s, SEG)
            mask = (inner >= lo) & (inner < hi)
            masks.append((jnp.where(pos[k], s - SEG, s + SEG), mask))
        frames.append((tiles, masks))
    for u in range(TILES + 2):
        base = u * EROW
        back = SEG * (u // TILES)
        shift = back + u % TILES
        for g in range(C // CP):
            rows = slice(base + g * CP, base + (g + 1) * CP)
            v = pltpu.roll(left, (2 * CC - shift - TILES * g) % CC, 1)
            xx[rows, :CC] = jnp.where(inner == 0, v, 0.0).astype(bf16)
            xx[rows, CC:] = zero
            rows = slice(base + C + g * CP, base + C + (g + 1) * CP)
            v = pltpu.roll(right, (2 * CC + SEG - 1 - shift - TILES * g) % CC, 1)
            xx[rows, :CC] = zero
            xx[rows, CC:] = jnp.where(inner == SEG - 1, v, 0.0).astype(bf16)
        for k in range(FRAMES):
            tiles, masks = frames[k]
            for j in range(3):
                move, mask = masks[j]
                v = pltpu.roll(tiles[u % TILES], (move - back + 2 * CC) % CC, 1)
                v = jnp.where(mask, v, 0.0).astype(bf16)
                at = base + 2 * C + j * FRAMES * CP + k * CP
                xx[at : at + CP, :CC] = jnp.where(pos[k], v, zero)
                xx[at : at + CP, CC:] = jnp.where(pos[k], zero, v)
    xx[(TILES + 2) * EROW :, :] = jnp.zeros((KEDGE - 3 * EROW, 2 * CC), bf16)
    for t in range(TILES):
        corr[t] = jnp.dot(
            wedge[...], xx[t * EROW : t * EROW + KEDGE, :], preferred_element_type=f32
        )
    wide = lanes((C // PARTS, CC))
    copies = []
    for n in range(PARTS):
        rows = slice(n * C // PARTS, (n + 1) * C // PARTS)
        for y in range(CR):
            q = y // TILES
            lft = pltpu.roll(corr[y % TILES, rows, :CC], (CC - SEG * q) % CC, 1)
            rgt = pltpu.roll(corr[y % TILES, rows, CC:], (SEG0 - SEG * q) % CC, 1)
            v = jnp.where(wide < SEG, lft, jnp.where(wide >= SEG0, rgt, 0.0))
            at = 0 if y < CR // 2 else CC
            v = jnp.maximum(part[y % (CR // 2), rows, at : at + CC] + v, 0.0)
            acc[pl.ds(n * C * CR // PARTS + y, C // PARTS, stride=CR), :] = v
        piece = pl.ds(n * C * CR // PARTS, C * CR // PARTS)
        done[piece] = acc[piece].astype(bf16)
        copies.append(pltpu.make_async_copy(done.at[piece], out.at[piece], sems.at[n]))
        copies[-1].start()
    for copy in copies:
        copy.wait()


def partner(i, size, shifted):
    if not shifted:
        return i ^ 1
    j = i - 1 if i % 2 == 0 else i + 1
    return j if 0 <= j < size else None


def swap(x, axis, shifted):
    nrows, ncols = lax.axis_size("rows"), lax.axis_size("cols")
    pairs = []
    for r in range(nrows):
        for c in range(ncols):
            if axis == "rows":
                to = partner(r, nrows, shifted)
                to = (r, c ^ 2) if to is None else (to, c)
            else:
                to = partner(c, ncols, shifted)
                to = (r ^ 1, c) if to is None else (r, to)
            pairs.append((r * ncols + c, to[0] * ncols + to[1]))
    return lax.ppermute(x, ("rows", "cols"), pairs)


def cost(flops, bytes_accessed):
    return pl.CostEstimate(flops=flops, bytes_accessed=bytes_accessed, transcendentals=0)


def call(kernel, outs, specs, scratch, estimate, place=None):
    vmem = pl.BlockSpec(memory_space=pltpu.VMEM)
    return pl.pallas_call(
        kernel,
        out_shape=[jax.ShapeDtypeStruct(*out) for out in outs],
        in_specs=specs,
        out_specs=[place or vmem] * len(outs),
        scratch_shapes=scratch,
        cost_estimate=estimate,
        compiler_params=pltpu.CompilerParams(vmem_limit_bytes=VMEM_LIMIT),
    )


def body(current_frame, history_frames, offsets, compress_weight, mixer_weight, mixer_bias):
    vmem = pl.BlockSpec(memory_space=pltpu.VMEM)
    hbm = pl.BlockSpec(memory_space=pltpu.HBM)
    off = offsets.T
    hist = history_frames.reshape(FRAMES, C * CR, CC)
    cur = current_frame.reshape(C * CR, CC)
    wt = mixer_weight.transpose(0, 1, 3, 2)
    nrows, ncols = lax.axis_size("rows"), lax.axis_size("cols")
    row_send = (2 * REACH + C // CP, CP, CC)
    col_send = (2 * TILES + 1, CP, CC)
    red, send_a, send_b = call(
        compress_kernel,
        [((FRAMES, CR, CP, CC), bf16), (row_send, bf16), (row_send, bf16)],
        [hbm] * 4,
        [
            pltpu.SMEM((2, FRAMES), jnp.int32),
            pltpu.VMEM((CP, C), bf16),
            pltpu.VMEM((FRAMES, C * CR, CC), bf16),
            pltpu.VMEM((C * CR, CC), bf16),
            pltpu.SemaphoreType.DMA((FRAMES + 3,)),
        ],
        cost(2 * FRAMES * CP * C * CR * CC, 3 << 20),
    )(*[pltpu.with_memory_space_constraint(v, pltpu.HBM) for v in (off, hist, cur, compress_weight)])
    recv_a = swap(send_a, "rows", False)
    recv_b = swap(send_b, "rows", True)
    cur_t, cols, wall, wedge = call(
        prepare_kernel,
        [((CR, C, CC), bf16), ((2, C, CC), bf16), ((C, KALL), bf16), ((C, KEDGE), bf16)],
        [vmem, vmem],
        [pltpu.VMEM((C * CR, CC), f32)],
        cost(1 << 20, 3 << 20),
    )(cur, wt)
    halo_rows = pltpu.VMEM((FRAMES, CR + 2 * REACH, CP, CC), bf16)
    csend_a, csend_b = call(
        lambda *refs: pack_kernel(nrows, *refs),
        [(col_send, bf16), (col_send, bf16)],
        [vmem] * 5,
        [halo_rows],
        cost(1 << 20, 2 << 20),
    )(off, red, recv_b, recv_a, cols)
    crecv_b = swap(csend_b, "cols", True)
    crecv_a = swap(csend_a, "cols", False)
    (part,) = call(
        lambda *refs: local_kernel(nrows, ncols, *refs),
        [((CR // 2, C, 2 * CC), f32)],
        [vmem] * 7,
        [halo_rows, pltpu.VMEM(((WIN - CR // 2) * KROW + KALL - 3 * KROW, 2 * CC), bf16)],
        cost(2 * C * KALL * CR * CC, 4 << 20),
    )(off, red, recv_b, recv_a, cur_t, wall, mixer_bias.reshape(C, 1))
    (out,) = call(
        lambda *refs: finish_kernel(ncols, *refs),
        [((C * CR, CC), bf16)],
        [vmem] * 5,
        [
            pltpu.VMEM(((TILES + 2) * EROW + KEDGE - 3 * EROW, 2 * CC), bf16),
            pltpu.VMEM((C * CR, CC), f32),
            pltpu.VMEM((TILES, C, 2 * CC), f32),
            pltpu.VMEM((C * CR, CC), bf16),
            pltpu.SemaphoreType.DMA((PARTS,)),
        ],
        cost(1 << 20, 2 << 20),
        hbm,
    )(off, crecv_b, crecv_a, part, wedge)
    return out.reshape(C, CR, CC)


def solution(mesh):
    in_specs = (P(None, "rows", "cols"), P(None, None, "rows", "cols"), P(), P(), P(), P())
    out_specs = P(None, "rows", "cols")
    return jax.shard_map(body, mesh=mesh, in_specs=in_specs, out_specs=out_specs, check_vma=False)
```

```python
import jax
import jax.numpy as jnp
from jax import lax
from jax.experimental import pallas as pl
from jax.experimental.pallas import tpu as pltpu
from jax.sharding import PartitionSpec as P

C = 128
CP = 32
FRAMES = 3
CR = 16
CC = 128
SHIFT_X = 16
SHIFT_Y = 8
REACH = SHIFT_Y + 1
PER = 6
EDGE = 5
LAST = 8
WIN = CR + 2
KROW = 3 * C + 3 * FRAMES * CP
KALL = 2048
PARTS = 4
EROW = 2 * C + 3 * FRAMES * CP
KEDGE = 1664
TILES = 3
SEG = 21
SEG0 = CC - SEG
VMEM_LIMIT = 48 * 1024 * 1024
f32 = jnp.float32
bf16 = jnp.bfloat16


def slots(off, axis):
    pos = [off[axis][k] > 0 for k in range(FRAMES)]
    first_pos = jnp.where(pos[0], 0, jnp.where(pos[1], 1, 2))
    last_pos = jnp.where(pos[2], 2, jnp.where(pos[1], 1, 0))
    first_neg = jnp.where(pos[0], jnp.where(pos[1], 2, 1), 0)
    last_neg = jnp.where(pos[2], jnp.where(pos[1], 0, 1), 2)
    place = [
        jnp.where(pos[k], jnp.where(first_pos == k, 0, 1), jnp.where(first_neg == k, 0, 1))
        for k in range(FRAMES)
    ]
    return pos, (first_pos, last_pos), (first_neg, last_neg), place


def scalars(ref):
    return [[ref[axis, k] for k in range(FRAMES)] for axis in range(2)]


def pick(values, k):
    return jnp.where(k == 0, values[0], jnp.where(k == 1, values[1], values[2]))


def lanes(shape):
    return lax.broadcasted_iota(jnp.int32, shape, len(shape) - 1)


def compress_kernel(
    off_hbm, hist, cur, w_hbm, red, edge_a, rows0_a, rows1_a, first_b, second_b, off, w, hbuf, cbuf, sems
):
    copies = [pltpu.make_async_copy(hist.at[k], hbuf.at[k], sems.at[k]) for k in range(FRAMES)]
    copies.append(pltpu.make_async_copy(cur, cbuf, sems.at[FRAMES]))
    small = [
        pltpu.make_async_copy(w_hbm, w, sems.at[FRAMES + 1]),
        pltpu.make_async_copy(off_hbm, off, sems.at[FRAMES + 2]),
    ]
    for copy in small[:1] + copies + small[1:]:
        copy.start()
    row = lax.axis_index("rows")
    even = row % 2 == 0
    small[0].wait()
    for k in range(FRAMES):
        copies[k].wait()
        by_row = jnp.swapaxes(hbuf[k].reshape(C, CR, CC), 0, 1)
        x = jnp.concatenate([by_row[y] for y in range(CR)], axis=1)
        r = jnp.dot(w[...], x, preferred_element_type=f32).astype(bf16)
        for y in range(CR):
            red[k, y] = r[:, y * CC : (y + 1) * CC]
    copies[FRAMES].wait()
    by_row = jnp.swapaxes(cbuf[...].reshape(C, CR, CC), 0, 1)
    top = by_row[0].reshape(C // CP, CP, CC)
    bottom = by_row[CR - 1].reshape(C // CP, CP, CC)
    small[1].wait()
    offs = scalars(off)
    _, posf, negf, _ = slots(offs, 0)
    lane = lanes((CP, CC))
    for (row0, row1, edge, at, tail, tail_at), down in (
        ((rows0_a, rows1_a, edge_a, 0, edge_a, EDGE), even),
        ((first_b, second_b, first_b, REACH, second_b, REACH), jnp.logical_not(even)),
    ):
        start = jnp.where(down, CR - REACH, 0)
        border = jnp.where(down, bottom, top)
        for s in range(2):
            k = jnp.where(down, posf[s], negf[s])
            back = jnp.where(pick(offs[1], k) > 0, SEG0, 0)
            for h in range(REACH):
                (row0, row1)[s][h] = red[k, start + h]
            for n in range(2):
                total = None
                for q in range(min(PER, REACH - PER * n)):
                    piece = red[k, start + PER * n + q].astype(f32)
                    piece = pltpu.roll(piece, (SEG * q - back + CC) % CC, 1)
                    total = piece if q == 0 else jnp.where(lane >= SEG * q, piece, total)
                edge[at + 2 * s + n] = total.astype(bf16)
        tail[tail_at : tail_at + C // CP] = border
        total = jnp.zeros((CP, CC), f32)
        for g in range(C // CP):
            piece = border[g].astype(f32)
            total = jnp.where(lane == g, pltpu.roll(piece, g, 1), total)
            total = jnp.where(lane == LAST + g, pltpu.roll(piece, LAST + g + 1, 1), total)
        edge[at + 4] = total.astype(bf16)


def spot(r):
    return SEG * (r // TILES) + r % TILES


def segment_lane(shape):
    lane = lanes(shape)
    base = jnp.zeros(shape, jnp.int32)
    for m in range(1, CC // SEG + 1):
        base = jnp.where(lane >= SEG * m, SEG * m, base)
    return lane - base


def prepare_kernel(cur, wt, cur_t, cols, wall, wedge, fbuf):
    fbuf[...] = cur[...].astype(f32)
    lane = lanes((C, CC))
    first = jnp.zeros((C, CC), f32)
    last = jnp.zeros((C, CC), f32)
    for y in range(CR):
        t = fbuf[pl.ds(y, C, stride=CR), :]
        cur_t[y] = t.astype(bf16)
        at = spot(y + 1)
        first = jnp.where(lane == at, pltpu.roll(t, at, 1), first)
        last = jnp.where(lane == at, pltpu.roll(t, at + 1, 1), last)
    cols[0] = first.astype(bf16)
    cols[1] = last.astype(bf16)
    for dest, taps, size in ((wall, (0, 1, 2), KALL), (wedge, (0, 2), KEDGE)):
        parts = []
        for i in range(3):
            parts += [wt[i, j, :C, :] for j in taps]
            parts += [wt[i, j, C:, :] for j in range(3)]
        parts.append(jnp.zeros((size - sum(p.shape[0] for p in parts), C), bf16))
        tall = jnp.concatenate(parts, axis=0).astype(f32)
        for b in range(size // C):
            dest[:, b * C : (b + 1) * C] = tall[b * C : (b + 1) * C].T.astype(bf16)


def row_halo(nrows, off, red, edge_a, rows0_a, rows1_a, first_b, second_b, cb):
    row = lax.axis_index("rows")
    even = row % 2 == 0
    has_above = row > 0
    has_below = row < nrows - 1
    pos, _, _, place = slots(off, 0)
    zero = jnp.zeros((REACH, CP, CC), bf16)
    for k in range(FRAMES):
        cb[k, REACH : REACH + CR] = red[k]
        from_a = jnp.where(place[k] == 0, rows0_a[...], rows1_a[...])
        from_b = jnp.where(place[k] == 0, first_b[:REACH], second_b[:REACH])
        use_a = jnp.logical_xor(pos[k], even)
        ok = jnp.where(pos[k], has_above, has_below)
        halo = jnp.where(ok, jnp.where(use_a, from_a, from_b), zero)
        cb[k, pl.ds(jnp.where(pos[k], 0, REACH + CR), REACH)] = halo
    tail_a = edge_a[EDGE:].reshape(C, CC)
    tail_b = second_b[REACH:].reshape(C, CC)
    blank = jnp.zeros((C, CC), bf16)
    above = jnp.where(has_above, jnp.where(even, tail_b, tail_a), blank)
    below = jnp.where(has_below, jnp.where(even, tail_a, tail_b), blank)
    return above, below, has_above, has_below


def window_row(dy, cb, k, r, has_above, has_below):
    v = cb[k, SHIFT_Y - dy + r]
    if r == 0:
        v = jnp.where(has_above, v, jnp.zeros_like(v))
    if r == WIN - 1:
        v = jnp.where(has_below, v, jnp.zeros_like(v))
    return v


def pack_kernel(nrows, off, red, first_b, edge_a, cols, send_a, send_b, cb):
    off = scalars(off)
    row = lax.axis_index("rows")
    even = row % 2 == 0
    has_above = row > 0
    has_below = row < nrows - 1
    _, _, _, place = slots(off, 0)
    zero = jnp.zeros((CP, CC), bf16)
    corner_a = edge_a[4]
    corner_b = first_b[REACH + 4]
    above = jnp.where(has_above, jnp.where(even, corner_b, corner_a), zero).astype(f32)
    below = jnp.where(has_below, jnp.where(even, corner_a, corner_b), zero).astype(f32)
    ceven = lax.axis_index("cols") % 2 == 0
    _, posf, negf, _ = slots(off, 1)
    lane = lanes((CP, CC))
    inner = segment_lane((CP, CC))
    end = spot(WIN - 1)

    def column(which, at):
        parts = []
        for g in range(C // CP):
            v = cols[which, CP * g : CP * (g + 1)].astype(f32)
            v = jnp.where(lane == 0, pltpu.roll(above, (CC - at - g) % CC, 1), v)
            v = jnp.where(lane == end, pltpu.roll(below, (CC + end - at - g) % CC, 1), v)
            parts.append(v)
        return parts

    first = column(0, 0)
    last = column(1, LAST)
    for send, right in ((send_a, ceven), (send_b, jnp.logical_not(ceven))):
        back = jnp.where(right, SEG0, 0)
        for s in range(2):
            k = jnp.where(right, posf[s], negf[s])
            dy = pick(off[0], k)
            before = dy > 0
            near = 2 * pick(place, k)
            use_a = jnp.logical_xor(before, even)
            ok = jnp.where(before, has_above, has_below)
            halo = []
            for n in range(2):
                v = jnp.where(use_a, edge_a[near + n], first_b[REACH + near + n])
                halo.append(jnp.where(ok, v, zero).astype(f32))
            n = 2 * (send is send_b) + s
            cb[n, REACH : REACH + CR] = red[k]
            at = jnp.where(before, 0, REACH + CR)
            for h in range(REACH):
                shift = (back - SEG * (h % PER) + CC) % CC
                cb[n, at + h] = pltpu.roll(halo[h // PER], shift, 1).astype(bf16)
            for t in range(TILES):
                total = None
                for q in range(WIN // TILES):
                    piece = window_row(dy, cb, n, t + TILES * q, has_above, has_below)
                    piece = pltpu.roll(piece.astype(f32), (SEG * q - back + CC) % CC, 1)
                    total = piece if q == 0 else jnp.where(lane >= SEG * q, piece, total)
                send[s * TILES + t] = total.astype(bf16)
        total = jnp.where(right, last[0], first[0])
        for g in range(1, C // CP):
            moved = pltpu.roll(jnp.where(right, last[g], first[g]), TILES * g, 1)
            total = jnp.where(inner >= TILES * g, moved, total)
        send[2 * TILES] = total.astype(bf16)


def local_kernel(
    nrows, ncols, off, red, first_b, second_b, edge_a, rows0_a, rows1_a, *rest
):
    cur_t, wall, bias, part, cb, x2 = rest
    off = scalars(off)
    above, below, has_above, has_below = row_halo(
        nrows, off, red, edge_a, rows0_a, rows1_a, first_b, second_b, cb
    )
    col = lax.axis_index("cols")
    has_left = col > 0
    has_right = col < ncols - 1
    pos, _, _, _ = slots(off, 1)
    lane = lanes((CP, CC))
    wide = lanes((C, CC))

    def put(r, at, size, value):
        if r <= WIN - CR // 2 - 1:
            x2[r * KROW + at : r * KROW + at + size, :CC] = value
        if r >= CR // 2:
            q = r - CR // 2
            x2[q * KROW + at : q * KROW + at + size, CC:] = value

    taps = []
    for k in range(FRAMES):
        for j in range(3):
            s = off[1][k] + 1 - j
            lo = jnp.where(pos[k], s, 0)
            hi = jnp.where(pos[k], CC, CC + s)
            if j == 0:
                lo = jnp.where(has_left, lo, jnp.maximum(lo, 1))
            if j == 2:
                hi = jnp.where(has_right, hi, jnp.minimum(hi, CC - 1))
            taps.append(((s + CC) % CC, (lane >= lo) & (lane < hi)))
    for r in range(WIN):
        here = above if r == 0 else below if r == WIN - 1 else cur_t[r - 1]
        put(r, C, C, here)
        here = here.astype(f32)
        zero = jnp.zeros_like(here)
        put(r, 0, C, jnp.where(wide == 0, zero, pltpu.roll(here, 1, 1)).astype(bf16))
        put(r, 2 * C, C, jnp.where(wide == CC - 1, zero, pltpu.roll(here, CC - 1, 1)).astype(bf16))
        for k in range(FRAMES):
            own = window_row(off[0][k], cb, k, r, has_above, has_below).astype(f32)
            for j in range(3):
                s, mask = taps[3 * k + j]
                v = jnp.where(mask, pltpu.roll(own, s, 1), jnp.zeros_like(own))
                put(r, 3 * C + j * FRAMES * CP + k * CP, CP, v.astype(bf16))
    x2[(WIN - CR // 2) * KROW :, :] = jnp.zeros((KALL - 3 * KROW, 2 * CC), bf16)
    bias_col = jnp.broadcast_to(bias[...], (C, 2 * CC))
    for y in range(CR // 2):
        p = jnp.dot(
            wall[...], x2[y * KROW : y * KROW + KALL, :], preferred_element_type=f32
        )
        part[y] = p + bias_col


def finish_kernel(ncols, off, recv_b, recv_a, part, wedge, out, xx, acc, corr, done, sems):
    off = scalars(off)
    col = lax.axis_index("cols")
    ceven = col % 2 == 0
    has_left = col > 0
    has_right = col < ncols - 1
    pos, _, _, place = slots(off, 1)
    inner = segment_lane((CP, CC))
    zero = jnp.zeros((CP, CC), bf16)
    cur_a = recv_a[2 * TILES].astype(f32)
    cur_b = recv_b[2 * TILES].astype(f32)
    left = jnp.where(ceven, cur_b, cur_a)
    right = jnp.where(ceven, cur_a, cur_b)
    left = jnp.where(has_left, left, jnp.zeros_like(left))
    right = jnp.where(has_right, right, jnp.zeros_like(right))
    frames = []
    for k in range(FRAMES):
        use_a = jnp.logical_xor(pos[k], ceven)
        ok = jnp.where(pos[k], has_left, has_right)
        tiles = []
        for t in range(TILES):
            v = jnp.where(use_a, recv_a[place[k] * TILES + t], recv_b[place[k] * TILES + t])
            tiles.append(jnp.where(ok, v, zero).astype(f32))
        masks = []
        for j in range(3):
            s = off[1][k] + 1 - j
            lo = jnp.where(pos[k], 0, SEG + s)
            hi = jnp.where(pos[k], s, SEG)
            mask = (inner >= lo) & (inner < hi)
            masks.append((jnp.where(pos[k], s - SEG, s + SEG), mask))
        frames.append((tiles, masks))
    for u in range(TILES + 2):
        base = u * EROW
        back = SEG * (u // TILES)
        shift = back + u % TILES
        for g in range(C // CP):
            rows = slice(base + g * CP, base + (g + 1) * CP)
            v = pltpu.roll(left, (2 * CC - shift - TILES * g) % CC, 1)
            xx[rows, :CC] = jnp.where(inner == 0, v, 0.0).astype(bf16)
            xx[rows, CC:] = zero
            rows = slice(base + C + g * CP, base + C + (g + 1) * CP)
            v = pltpu.roll(right, (2 * CC + SEG - 1 - shift - TILES * g) % CC, 1)
            xx[rows, :CC] = zero
            xx[rows, CC:] = jnp.where(inner == SEG - 1, v, 0.0).astype(bf16)
        for k in range(FRAMES):
            tiles, masks = frames[k]
            for j in range(3):
                move, mask = masks[j]
                v = pltpu.roll(tiles[u % TILES], (move - back + 2 * CC) % CC, 1)
                v = jnp.where(mask, v, 0.0).astype(bf16)
                at = base + 2 * C + j * FRAMES * CP + k * CP
                xx[at : at + CP, :CC] = jnp.where(pos[k], v, zero)
                xx[at : at + CP, CC:] = jnp.where(pos[k], zero, v)
    xx[(TILES + 2) * EROW :, :] = jnp.zeros((KEDGE - 3 * EROW, 2 * CC), bf16)
    for t in range(TILES):
        corr[t] = jnp.dot(
            wedge[...], xx[t * EROW : t * EROW + KEDGE, :], preferred_element_type=f32
        )
    wide = lanes((C // PARTS, CC))
    copies = []
    for n in range(PARTS):
        rows = slice(n * C // PARTS, (n + 1) * C // PARTS)
        for y in range(CR):
            q = y // TILES
            lft = pltpu.roll(corr[y % TILES, rows, :CC], (CC - SEG * q) % CC, 1)
            rgt = pltpu.roll(corr[y % TILES, rows, CC:], (SEG0 - SEG * q) % CC, 1)
            v = jnp.where(wide < SEG, lft, jnp.where(wide >= SEG0, rgt, 0.0))
            at = 0 if y < CR // 2 else CC
            v = jnp.maximum(part[y % (CR // 2), rows, at : at + CC] + v, 0.0)
            acc[pl.ds(n * C * CR // PARTS + y, C // PARTS, stride=CR), :] = v
        piece = pl.ds(n * C * CR // PARTS, C * CR // PARTS)
        done[piece] = acc[piece].astype(bf16)
        copies.append(pltpu.make_async_copy(done.at[piece], out.at[piece], sems.at[n]))
        copies[-1].start()
    for copy in copies:
        copy.wait()


def partner(i, size, shifted):
    if not shifted:
        return i ^ 1
    j = i - 1 if i % 2 == 0 else i + 1
    return j if 0 <= j < size else None


def swap(x, axis, shifted):
    nrows, ncols = lax.axis_size("rows"), lax.axis_size("cols")
    pairs = []
    for r in range(nrows):
        for c in range(ncols):
            if axis == "rows":
                to = partner(r, nrows, shifted)
                to = (r, c ^ 2) if to is None else (to, c)
            else:
                to = partner(c, ncols, shifted)
                to = (r ^ 1, c) if to is None else (r, to)
            pairs.append((r * ncols + c, to[0] * ncols + to[1]))
    return lax.ppermute(x, ("rows", "cols"), pairs)


def cost(flops, bytes_accessed):
    return pl.CostEstimate(flops=flops, bytes_accessed=bytes_accessed, transcendentals=0)


def call(kernel, outs, specs, scratch, estimate, place=None):
    vmem = pl.BlockSpec(memory_space=pltpu.VMEM)
    return pl.pallas_call(
        kernel,
        out_shape=[jax.ShapeDtypeStruct(*out) for out in outs],
        in_specs=specs,
        out_specs=[place or vmem] * len(outs),
        scratch_shapes=scratch,
        cost_estimate=estimate,
        compiler_params=pltpu.CompilerParams(vmem_limit_bytes=VMEM_LIMIT),
    )


def body(current_frame, history_frames, offsets, compress_weight, mixer_weight, mixer_bias):
    vmem = pl.BlockSpec(memory_space=pltpu.VMEM)
    hbm = pl.BlockSpec(memory_space=pltpu.HBM)
    off = offsets.T
    hist = history_frames.reshape(FRAMES, C * CR, CC)
    cur = current_frame.reshape(C * CR, CC)
    wt = mixer_weight.transpose(0, 1, 3, 2)
    nrows, ncols = lax.axis_size("rows"), lax.axis_size("cols")
    col_send = (2 * TILES + 1, CP, CC)
    red, edge_a, rows0_a, rows1_a, first_b, second_b = call(
        compress_kernel,
        [
            ((FRAMES, CR, CP, CC), bf16),
            ((EDGE + C // CP, CP, CC), bf16),
            ((REACH, CP, CC), bf16),
            ((REACH, CP, CC), bf16),
            ((REACH + EDGE, CP, CC), bf16),
            ((REACH + C // CP, CP, CC), bf16),
        ],
        [hbm] * 4,
        [
            pltpu.SMEM((2, FRAMES), jnp.int32),
            pltpu.VMEM((CP, C), bf16),
            pltpu.VMEM((FRAMES, C * CR, CC), bf16),
            pltpu.VMEM((C * CR, CC), bf16),
            pltpu.SemaphoreType.DMA((FRAMES + 3,)),
        ],
        cost(2 * FRAMES * CP * C * CR * CC, 3 << 20),
    )(*[pltpu.with_memory_space_constraint(v, pltpu.HBM) for v in (off, hist, cur, compress_weight)])
    edge_a = swap(edge_a, "rows", False)
    rows0_a = swap(rows0_a, "rows", False)
    rows1_a = swap(rows1_a, "rows", False)
    first_b = swap(first_b, "rows", True)
    second_b = swap(second_b, "rows", True)
    cur_t, cols, wall, wedge = call(
        prepare_kernel,
        [((CR, C, CC), bf16), ((2, C, CC), bf16), ((C, KALL), bf16), ((C, KEDGE), bf16)],
        [vmem, vmem],
        [pltpu.VMEM((C * CR, CC), f32)],
        cost(1 << 20, 3 << 20),
    )(cur, wt)
    halo_rows = pltpu.VMEM((FRAMES, CR + 2 * REACH, CP, CC), bf16)
    csend_a, csend_b = call(
        lambda *refs: pack_kernel(nrows, *refs),
        [(col_send, bf16), (col_send, bf16)],
        [vmem] * 5,
        [pltpu.VMEM((4, CR + 2 * REACH, CP, CC), bf16)],
        cost(1 << 20, 2 << 20),
    )(off, red, first_b, edge_a, cols)
    crecv_b = swap(csend_b, "cols", True)
    crecv_a = swap(csend_a, "cols", False)
    (part,) = call(
        lambda *refs: local_kernel(nrows, ncols, *refs),
        [((CR // 2, C, 2 * CC), f32)],
        [vmem] * 10,
        [halo_rows, pltpu.VMEM(((WIN - CR // 2) * KROW + KALL - 3 * KROW, 2 * CC), bf16)],
        cost(2 * C * KALL * CR * CC, 4 << 20),
    )(off, red, first_b, second_b, edge_a, rows0_a, rows1_a, cur_t, wall, mixer_bias.reshape(C, 1))
    (out,) = call(
        lambda *refs: finish_kernel(ncols, *refs),
        [((C * CR, CC), bf16)],
        [vmem] * 5,
        [
            pltpu.VMEM(((TILES + 2) * EROW + KEDGE - 3 * EROW, 2 * CC), bf16),
            pltpu.VMEM((C * CR, CC), f32),
            pltpu.VMEM((TILES, C, 2 * CC), f32),
            pltpu.VMEM((C * CR, CC), bf16),
            pltpu.SemaphoreType.DMA((PARTS,)),
        ],
        cost(1 << 20, 2 << 20),
        hbm,
    )(off, crecv_b, crecv_a, part, wedge)
    return out.reshape(C, CR, CC)


def solution(mesh):
    in_specs = (P(None, "rows", "cols"), P(None, None, "rows", "cols"), P(), P(), P(), P())
    out_specs = P(None, "rows", "cols")
    return jax.shard_map(body, mesh=mesh, in_specs=in_specs, out_specs=out_specs, check_vma=False)
```

```python
import jax
import jax.numpy as jnp
from jax import lax
from jax.experimental import pallas as pl
from jax.experimental.pallas import tpu as pltpu
from jax.sharding import PartitionSpec as P

C = 128
CP = 32
FRAMES = 3
CR = 16
CC = 128
SHIFT_X = 16
SHIFT_Y = 8
REACH = SHIFT_Y + 1
PER = 6
EDGE = 5
LAST = 8
WIN = CR + 2
KROW = 3 * C + 3 * FRAMES * CP
KALL = 2048
PARTS = 8
EROW = 2 * C + 3 * FRAMES * CP
KEDGE = 1664
TILES = 3
SEG = 21
SEG0 = CC - SEG
VMEM_LIMIT = 48 * 1024 * 1024
f32 = jnp.float32
bf16 = jnp.bfloat16


def slots(off, axis):
    pos = [off[axis][k] > 0 for k in range(FRAMES)]
    first_pos = jnp.where(pos[0], 0, jnp.where(pos[1], 1, 2))
    last_pos = jnp.where(pos[2], 2, jnp.where(pos[1], 1, 0))
    first_neg = jnp.where(pos[0], jnp.where(pos[1], 2, 1), 0)
    last_neg = jnp.where(pos[2], jnp.where(pos[1], 0, 1), 2)
    place = [
        jnp.where(pos[k], jnp.where(first_pos == k, 0, 1), jnp.where(first_neg == k, 0, 1))
        for k in range(FRAMES)
    ]
    return pos, (first_pos, last_pos), (first_neg, last_neg), place


def scalars(ref):
    return [[ref[axis, k] for k in range(FRAMES)] for axis in range(2)]


def pick(values, k):
    return jnp.where(k == 0, values[0], jnp.where(k == 1, values[1], values[2]))


def lanes(shape):
    return lax.broadcasted_iota(jnp.int32, shape, len(shape) - 1)


def compress_kernel(
    off_hbm, hist, cur, w_hbm, red, edge_a, rows0_a, rows1_a, first_b, second_b, off, w, hbuf, cbuf, sems
):
    copies = [pltpu.make_async_copy(hist.at[k], hbuf.at[k], sems.at[k]) for k in range(FRAMES)]
    copies.append(pltpu.make_async_copy(cur, cbuf, sems.at[FRAMES]))
    small = [
        pltpu.make_async_copy(w_hbm, w, sems.at[FRAMES + 1]),
        pltpu.make_async_copy(off_hbm, off, sems.at[FRAMES + 2]),
    ]
    for copy in small[:1] + copies + small[1:]:
        copy.start()
    row = lax.axis_index("rows")
    even = row % 2 == 0
    small[0].wait()
    for k in range(FRAMES):
        copies[k].wait()
        by_row = jnp.swapaxes(hbuf[k].reshape(C, CR, CC), 0, 1)
        x = jnp.concatenate([by_row[y] for y in range(CR)], axis=1)
        r = jnp.dot(w[...], x, preferred_element_type=f32).astype(bf16)
        for y in range(CR):
            red[k, y] = r[:, y * CC : (y + 1) * CC]
    copies[FRAMES].wait()
    by_row = jnp.swapaxes(cbuf[...].reshape(C, CR, CC), 0, 1)
    top = by_row[0].reshape(C // CP, CP, CC)
    bottom = by_row[CR - 1].reshape(C // CP, CP, CC)
    small[1].wait()
    offs = scalars(off)
    _, posf, negf, _ = slots(offs, 0)
    lane = lanes((CP, CC))
    for (row0, row1, edge, at, tail, tail_at), down in (
        ((rows0_a, rows1_a, edge_a, 0, edge_a, EDGE), even),
        ((first_b, second_b, first_b, REACH, second_b, REACH), jnp.logical_not(even)),
    ):
        start = jnp.where(down, CR - REACH, 0)
        border = jnp.where(down, bottom, top)
        for s in range(2):
            k = jnp.where(down, posf[s], negf[s])
            back = jnp.where(pick(offs[1], k) > 0, SEG0, 0)
            for h in range(REACH):
                (row0, row1)[s][h] = red[k, start + h]
            for n in range(2):
                total = None
                for q in range(min(PER, REACH - PER * n)):
                    piece = red[k, start + PER * n + q].astype(f32)
                    piece = pltpu.roll(piece, (SEG * q - back + CC) % CC, 1)
                    total = piece if q == 0 else jnp.where(lane >= SEG * q, piece, total)
                edge[at + 2 * s + n] = total.astype(bf16)
        tail[tail_at : tail_at + C // CP] = border
        total = jnp.zeros((CP, CC), f32)
        for g in range(C // CP):
            piece = border[g].astype(f32)
            total = jnp.where(lane == g, pltpu.roll(piece, g, 1), total)
            total = jnp.where(lane == LAST + g, pltpu.roll(piece, LAST + g + 1, 1), total)
        edge[at + 4] = total.astype(bf16)


def spot(r):
    return SEG * (r // TILES) + r % TILES


def segment_lane(shape):
    lane = lanes(shape)
    base = jnp.zeros(shape, jnp.int32)
    for m in range(1, CC // SEG + 1):
        base = jnp.where(lane >= SEG * m, SEG * m, base)
    return lane - base


def prepare_kernel(cur, wt, cur_t, cols, wall, wedge, fbuf):
    fbuf[...] = cur[...].astype(f32)
    lane = lanes((C, CC))
    first = jnp.zeros((C, CC), f32)
    last = jnp.zeros((C, CC), f32)
    for y in range(CR):
        t = fbuf[pl.ds(y, C, stride=CR), :]
        cur_t[y] = t.astype(bf16)
        at = spot(y + 1)
        first = jnp.where(lane == at, pltpu.roll(t, at, 1), first)
        last = jnp.where(lane == at, pltpu.roll(t, at + 1, 1), last)
    cols[0] = first.astype(bf16)
    cols[1] = last.astype(bf16)
    for dest, taps, size in ((wall, (0, 1, 2), KALL), (wedge, (0, 2), KEDGE)):
        parts = []
        for i in range(3):
            parts += [wt[i, j, :C, :] for j in taps]
            parts += [wt[i, j, C:, :] for j in range(3)]
        parts.append(jnp.zeros((size - sum(p.shape[0] for p in parts), C), bf16))
        tall = jnp.concatenate(parts, axis=0).astype(f32)
        for b in range(size // C):
            dest[:, b * C : (b + 1) * C] = tall[b * C : (b + 1) * C].T.astype(bf16)


def row_halo(nrows, off, red, edge_a, rows0_a, rows1_a, first_b, second_b, cb):
    row = lax.axis_index("rows")
    even = row % 2 == 0
    has_above = row > 0
    has_below = row < nrows - 1
    pos, _, _, place = slots(off, 0)
    zero = jnp.zeros((REACH, CP, CC), bf16)
    for k in range(FRAMES):
        cb[k, REACH : REACH + CR] = red[k]
        from_a = jnp.where(place[k] == 0, rows0_a[...], rows1_a[...])
        from_b = jnp.where(place[k] == 0, first_b[:REACH], second_b[:REACH])
        use_a = jnp.logical_xor(pos[k], even)
        ok = jnp.where(pos[k], has_above, has_below)
        halo = jnp.where(ok, jnp.where(use_a, from_a, from_b), zero)
        cb[k, pl.ds(jnp.where(pos[k], 0, REACH + CR), REACH)] = halo
    tail_a = edge_a[EDGE:].reshape(C, CC)
    tail_b = second_b[REACH:].reshape(C, CC)
    blank = jnp.zeros((C, CC), bf16)
    above = jnp.where(has_above, jnp.where(even, tail_b, tail_a), blank)
    below = jnp.where(has_below, jnp.where(even, tail_a, tail_b), blank)
    return above, below, has_above, has_below


def window_row(dy, cb, k, r, has_above, has_below):
    v = cb[k, SHIFT_Y - dy + r]
    if r == 0:
        v = jnp.where(has_above, v, jnp.zeros_like(v))
    if r == WIN - 1:
        v = jnp.where(has_below, v, jnp.zeros_like(v))
    return v


def pack_kernel(nrows, off, red, first_b, edge_a, cols, send_a, send_b, cb):
    off = scalars(off)
    row = lax.axis_index("rows")
    even = row % 2 == 0
    has_above = row > 0
    has_below = row < nrows - 1
    _, _, _, place = slots(off, 0)
    zero = jnp.zeros((CP, CC), bf16)
    corner_a = edge_a[4]
    corner_b = first_b[REACH + 4]
    above = jnp.where(has_above, jnp.where(even, corner_b, corner_a), zero).astype(f32)
    below = jnp.where(has_below, jnp.where(even, corner_a, corner_b), zero).astype(f32)
    ceven = lax.axis_index("cols") % 2 == 0
    _, posf, negf, _ = slots(off, 1)
    lane = lanes((CP, CC))
    inner = segment_lane((CP, CC))
    end = spot(WIN - 1)

    def column(which, at):
        parts = []
        for g in range(C // CP):
            v = cols[which, CP * g : CP * (g + 1)].astype(f32)
            v = jnp.where(lane == 0, pltpu.roll(above, (CC - at - g) % CC, 1), v)
            v = jnp.where(lane == end, pltpu.roll(below, (CC + end - at - g) % CC, 1), v)
            parts.append(v)
        return parts

    first = column(0, 0)
    last = column(1, LAST)
    for send, right in ((send_a, ceven), (send_b, jnp.logical_not(ceven))):
        back = jnp.where(right, SEG0, 0)
        for s in range(2):
            k = jnp.where(right, posf[s], negf[s])
            dy = pick(off[0], k)
            before = dy > 0
            near = 2 * pick(place, k)
            use_a = jnp.logical_xor(before, even)
            ok = jnp.where(before, has_above, has_below)
            halo = []
            for n in range(2):
                v = jnp.where(use_a, edge_a[near + n], first_b[REACH + near + n])
                halo.append(jnp.where(ok, v, zero).astype(f32))
            n = 2 * (send is send_b) + s
            cb[n, REACH : REACH + CR] = red[k]
            at = jnp.where(before, 0, REACH + CR)
            for h in range(REACH):
                shift = (back - SEG * (h % PER) + CC) % CC
                cb[n, at + h] = pltpu.roll(halo[h // PER], shift, 1).astype(bf16)
            for t in range(TILES):
                total = None
                for q in range(WIN // TILES):
                    piece = window_row(dy, cb, n, t + TILES * q, has_above, has_below)
                    piece = pltpu.roll(piece.astype(f32), (SEG * q - back + CC) % CC, 1)
                    total = piece if q == 0 else jnp.where(lane >= SEG * q, piece, total)
                send[s * TILES + t] = total.astype(bf16)
        total = jnp.where(right, last[0], first[0])
        for g in range(1, C // CP):
            moved = pltpu.roll(jnp.where(right, last[g], first[g]), TILES * g, 1)
            total = jnp.where(inner >= TILES * g, moved, total)
        send[2 * TILES] = total.astype(bf16)


def local_kernel(
    nrows, ncols, off, red, first_b, second_b, edge_a, rows0_a, rows1_a, *rest
):
    cur_t, wall, bias, part, cb, x2 = rest
    off = scalars(off)
    above, below, has_above, has_below = row_halo(
        nrows, off, red, edge_a, rows0_a, rows1_a, first_b, second_b, cb
    )
    col = lax.axis_index("cols")
    has_left = col > 0
    has_right = col < ncols - 1
    pos, _, _, _ = slots(off, 1)
    lane = lanes((CP, CC))
    wide = lanes((C, CC))

    def put(r, at, size, value):
        if r <= WIN - CR // 2 - 1:
            x2[r * KROW + at : r * KROW + at + size, :CC] = value
        if r >= CR // 2:
            q = r - CR // 2
            x2[q * KROW + at : q * KROW + at + size, CC:] = value

    taps = []
    for k in range(FRAMES):
        for j in range(3):
            s = off[1][k] + 1 - j
            lo = jnp.where(pos[k], s, 0)
            hi = jnp.where(pos[k], CC, CC + s)
            if j == 0:
                lo = jnp.where(has_left, lo, jnp.maximum(lo, 1))
            if j == 2:
                hi = jnp.where(has_right, hi, jnp.minimum(hi, CC - 1))
            taps.append(((s + CC) % CC, (lane >= lo) & (lane < hi)))
    for r in range(WIN):
        here = above if r == 0 else below if r == WIN - 1 else cur_t[r - 1]
        put(r, C, C, here)
        here = here.astype(f32)
        zero = jnp.zeros_like(here)
        put(r, 0, C, jnp.where(wide == 0, zero, pltpu.roll(here, 1, 1)).astype(bf16))
        put(r, 2 * C, C, jnp.where(wide == CC - 1, zero, pltpu.roll(here, CC - 1, 1)).astype(bf16))
        for k in range(FRAMES):
            own = window_row(off[0][k], cb, k, r, has_above, has_below).astype(f32)
            for j in range(3):
                s, mask = taps[3 * k + j]
                v = jnp.where(mask, pltpu.roll(own, s, 1), jnp.zeros_like(own))
                put(r, 3 * C + j * FRAMES * CP + k * CP, CP, v.astype(bf16))
    x2[(WIN - CR // 2) * KROW :, :] = jnp.zeros((KALL - 3 * KROW, 2 * CC), bf16)
    bias_col = jnp.broadcast_to(bias[...], (C, 2 * CC))
    for y in range(CR // 2):
        p = jnp.dot(
            wall[...], x2[y * KROW : y * KROW + KALL, :], preferred_element_type=f32
        )
        part[y] = p + bias_col


def finish_kernel(ncols, off, recv_b, recv_a, part, wedge, out, xx, acc, corr, done, sems):
    off = scalars(off)
    col = lax.axis_index("cols")
    ceven = col % 2 == 0
    has_left = col > 0
    has_right = col < ncols - 1
    pos, _, _, place = slots(off, 1)
    inner = segment_lane((CP, CC))
    zero = jnp.zeros((CP, CC), bf16)
    cur_a = recv_a[2 * TILES].astype(f32)
    cur_b = recv_b[2 * TILES].astype(f32)
    left = jnp.where(ceven, cur_b, cur_a)
    right = jnp.where(ceven, cur_a, cur_b)
    left = jnp.where(has_left, left, jnp.zeros_like(left))
    right = jnp.where(has_right, right, jnp.zeros_like(right))
    frames = []
    for k in range(FRAMES):
        use_a = jnp.logical_xor(pos[k], ceven)
        ok = jnp.where(pos[k], has_left, has_right)
        tiles = []
        for t in range(TILES):
            v = jnp.where(use_a, recv_a[place[k] * TILES + t], recv_b[place[k] * TILES + t])
            tiles.append(jnp.where(ok, v, zero).astype(f32))
        masks = []
        for j in range(3):
            s = off[1][k] + 1 - j
            lo = jnp.where(pos[k], 0, SEG + s)
            hi = jnp.where(pos[k], s, SEG)
            mask = (inner >= lo) & (inner < hi)
            masks.append((jnp.where(pos[k], s - SEG, s + SEG), mask))
        frames.append((tiles, masks))
    for u in range(TILES + 2):
        base = u * EROW
        back = SEG * (u // TILES)
        shift = back + u % TILES
        for g in range(C // CP):
            rows = slice(base + g * CP, base + (g + 1) * CP)
            v = pltpu.roll(left, (2 * CC - shift - TILES * g) % CC, 1)
            xx[rows, :CC] = jnp.where(inner == 0, v, 0.0).astype(bf16)
            xx[rows, CC:] = zero
            rows = slice(base + C + g * CP, base + C + (g + 1) * CP)
            v = pltpu.roll(right, (2 * CC + SEG - 1 - shift - TILES * g) % CC, 1)
            xx[rows, :CC] = zero
            xx[rows, CC:] = jnp.where(inner == SEG - 1, v, 0.0).astype(bf16)
        for k in range(FRAMES):
            tiles, masks = frames[k]
            for j in range(3):
                move, mask = masks[j]
                v = pltpu.roll(tiles[u % TILES], (move - back + 2 * CC) % CC, 1)
                v = jnp.where(mask, v, 0.0).astype(bf16)
                at = base + 2 * C + j * FRAMES * CP + k * CP
                xx[at : at + CP, :CC] = jnp.where(pos[k], v, zero)
                xx[at : at + CP, CC:] = jnp.where(pos[k], zero, v)
    xx[(TILES + 2) * EROW :, :] = jnp.zeros((KEDGE - 3 * EROW, 2 * CC), bf16)
    for t in range(TILES):
        corr[t] = jnp.dot(
            wedge[...], xx[t * EROW : t * EROW + KEDGE, :], preferred_element_type=f32
        )
    wide = lanes((C // PARTS, CC))
    copies = []
    for n in range(PARTS):
        rows = slice(n * C // PARTS, (n + 1) * C // PARTS)
        for y in range(CR):
            q = y // TILES
            lft = pltpu.roll(corr[y % TILES, rows, :CC], (CC - SEG * q) % CC, 1)
            rgt = pltpu.roll(corr[y % TILES, rows, CC:], (SEG0 - SEG * q) % CC, 1)
            v = jnp.where(wide < SEG, lft, jnp.where(wide >= SEG0, rgt, 0.0))
            at = 0 if y < CR // 2 else CC
            v = jnp.maximum(part[y % (CR // 2), rows, at : at + CC] + v, 0.0)
            acc[pl.ds(n * C * CR // PARTS + y, C // PARTS, stride=CR), :] = v
        piece = pl.ds(n * C * CR // PARTS, C * CR // PARTS)
        done[piece] = acc[piece].astype(bf16)
        copies.append(pltpu.make_async_copy(done.at[piece], out.at[piece], sems.at[n]))
        copies[-1].start()
    for copy in copies:
        copy.wait()


def partner(i, size, shifted):
    if not shifted:
        return i ^ 1
    j = i - 1 if i % 2 == 0 else i + 1
    return j if 0 <= j < size else None


def swap(x, axis, shifted):
    nrows, ncols = lax.axis_size("rows"), lax.axis_size("cols")
    pairs = []
    for r in range(nrows):
        for c in range(ncols):
            if axis == "rows":
                to = partner(r, nrows, shifted)
                to = (r, c ^ 2) if to is None else (to, c)
            else:
                to = partner(c, ncols, shifted)
                to = (r ^ 1, c) if to is None else (r, to)
            pairs.append((r * ncols + c, to[0] * ncols + to[1]))
    return lax.ppermute(x, ("rows", "cols"), pairs)


def cost(flops, bytes_accessed):
    return pl.CostEstimate(flops=flops, bytes_accessed=bytes_accessed, transcendentals=0)


def call(kernel, outs, specs, scratch, estimate, place=None):
    vmem = pl.BlockSpec(memory_space=pltpu.VMEM)
    return pl.pallas_call(
        kernel,
        out_shape=[jax.ShapeDtypeStruct(*out) for out in outs],
        in_specs=specs,
        out_specs=[place or vmem] * len(outs),
        scratch_shapes=scratch,
        cost_estimate=estimate,
        compiler_params=pltpu.CompilerParams(vmem_limit_bytes=VMEM_LIMIT),
    )


def body(current_frame, history_frames, offsets, compress_weight, mixer_weight, mixer_bias):
    vmem = pl.BlockSpec(memory_space=pltpu.VMEM)
    hbm = pl.BlockSpec(memory_space=pltpu.HBM)
    off = offsets.T
    hist = history_frames.reshape(FRAMES, C * CR, CC)
    cur = current_frame.reshape(C * CR, CC)
    wt = mixer_weight.transpose(0, 1, 3, 2)
    nrows, ncols = lax.axis_size("rows"), lax.axis_size("cols")
    col_send = (2 * TILES + 1, CP, CC)
    red, edge_a, rows0_a, rows1_a, first_b, second_b = call(
        compress_kernel,
        [
            ((FRAMES, CR, CP, CC), bf16),
            ((EDGE + C // CP, CP, CC), bf16),
            ((REACH, CP, CC), bf16),
            ((REACH, CP, CC), bf16),
            ((REACH + EDGE, CP, CC), bf16),
            ((REACH + C // CP, CP, CC), bf16),
        ],
        [hbm] * 4,
        [
            pltpu.SMEM((2, FRAMES), jnp.int32),
            pltpu.VMEM((CP, C), bf16),
            pltpu.VMEM((FRAMES, C * CR, CC), bf16),
            pltpu.VMEM((C * CR, CC), bf16),
            pltpu.SemaphoreType.DMA((FRAMES + 3,)),
        ],
        cost(2 * FRAMES * CP * C * CR * CC, 3 << 20),
    )(*[pltpu.with_memory_space_constraint(v, pltpu.HBM) for v in (off, hist, cur, compress_weight)])
    edge_a = swap(edge_a, "rows", False)
    rows0_a = swap(rows0_a, "rows", False)
    rows1_a = swap(rows1_a, "rows", False)
    first_b = swap(first_b, "rows", True)
    second_b = swap(second_b, "rows", True)
    cur_t, cols, wall, wedge = call(
        prepare_kernel,
        [((CR, C, CC), bf16), ((2, C, CC), bf16), ((C, KALL), bf16), ((C, KEDGE), bf16)],
        [vmem, vmem],
        [pltpu.VMEM((C * CR, CC), f32)],
        cost(1 << 20, 3 << 20),
    )(cur, wt)
    halo_rows = pltpu.VMEM((FRAMES, CR + 2 * REACH, CP, CC), bf16)
    csend_a, csend_b = call(
        lambda *refs: pack_kernel(nrows, *refs),
        [(col_send, bf16), (col_send, bf16)],
        [vmem] * 5,
        [pltpu.VMEM((4, CR + 2 * REACH, CP, CC), bf16)],
        cost(1 << 20, 2 << 20),
    )(off, red, first_b, edge_a, cols)
    crecv_b = swap(csend_b, "cols", True)
    crecv_a = swap(csend_a, "cols", False)
    (part,) = call(
        lambda *refs: local_kernel(nrows, ncols, *refs),
        [((CR // 2, C, 2 * CC), f32)],
        [vmem] * 10,
        [halo_rows, pltpu.VMEM(((WIN - CR // 2) * KROW + KALL - 3 * KROW, 2 * CC), bf16)],
        cost(2 * C * KALL * CR * CC, 4 << 20),
    )(off, red, first_b, second_b, edge_a, rows0_a, rows1_a, cur_t, wall, mixer_bias.reshape(C, 1))
    (out,) = call(
        lambda *refs: finish_kernel(ncols, *refs),
        [((C * CR, CC), bf16)],
        [vmem] * 5,
        [
            pltpu.VMEM(((TILES + 2) * EROW + KEDGE - 3 * EROW, 2 * CC), bf16),
            pltpu.VMEM((C * CR, CC), f32),
            pltpu.VMEM((TILES, C, 2 * CC), f32),
            pltpu.VMEM((C * CR, CC), bf16),
            pltpu.SemaphoreType.DMA((PARTS,)),
        ],
        cost(1 << 20, 2 << 20),
        hbm,
    )(off, crecv_b, crecv_a, part, wedge)
    return out.reshape(C, CR, CC)


def solution(mesh):
    in_specs = (P(None, "rows", "cols"), P(None, None, "rows", "cols"), P(), P(), P(), P())
    out_specs = P(None, "rows", "cols")
    return jax.shard_map(body, mesh=mesh, in_specs=in_specs, out_specs=out_specs, check_vma=False)
```
